32 devices in a mesh: dp: 8 (over y, x, core), tensor: 4 (over z).
Axes of the slice: x: 2, y: 2, z: 4, core: 2. Of those that a mesh axis runs over, the one named last changes fastest.
Arguments:
- tokens: bfloat16 [8192, 2048], P(('dp', 'tensor')), may hold values from -6 to 6
- segments: int32 [8192], P('dp'), may hold values from 0 to 1023, as said below
- positions: int32 [8192], P('dp'), may hold values from 0 to 1023, as said below
- norm_attn: float32 [2048], replicated, may hold values from 0.25 to 1.75
- w_query: bfloat16 [2048, 2048], P('dp', 'tensor'), may hold values from -0.125 to 0.125
- w_key: bfloat16 [2048, 512], P('dp', 'tensor'), may hold values from -0.125 to 0.125
- w_value: bfloat16 [2048, 512], P('dp', 'tensor'), may hold values from -0.125 to 0.125
- w_out: bfloat16 [2048, 2048], P('tensor', 'dp'), may hold values from -0.375 to 0.375
- norm_mlp: float32 [2048], replicated, may hold values from 0.25 to 1.75
- w_gate: bfloat16 [2048, 8192], P('dp', 'tensor'), may hold values from -0.125 to 0.125
- w_up: bfloat16 [2048, 8192], P('dp', 'tensor'), may hold values from -0.125 to 0.125
- w_down: bfloat16 [8192, 2048], P('tensor', 'dp'), may hold values from -0.09375 to 0.09375
- cotangent: bfloat16 [8192, 2048], P(('dp', 'tensor')), may hold values from -6 to 6
Outputs:
- layer_out: bfloat16 [8192, 2048], P(('dp', 'tensor'))
- input_grad: float32 [8192, 2048], P(('dp', 'tensor'))
- grad_norm_attn: float32 [2048], replicated
- grad_query: float32 [2048, 2048], P('dp', 'tensor')
- grad_key: float32 [2048, 512], P('dp', 'tensor')
- grad_value: float32 [2048, 512], P('dp', 'tensor')
- grad_output: float32 [2048, 2048], P('tensor', 'dp')
- grad_norm_mlp: float32 [2048], replicated
- grad_gate: float32 [2048, 8192], P('dp', 'tensor')
- grad_up: float32 [2048, 8192], P('dp', 'tensor')
- grad_down: float32 [8192, 2048], P('tensor', 'dp')
The draws below stay inside these ranges and needn't reach their ends.
Inputs may be any that keep to these rules, and one draw needn't show every extreme that they name: `segments`: within each sequence of 1024 tokens, a token's label is the place in that sequence of its document's first token, so labels never fall along a sequence; the first sequence of all is a single document, and the last token of the last sequence starts a document of its own. `positions`: each token's position counts from 0 at its document's first token.
All inputs are finite; a program needn't handle non-finite values.
Results may differ from the reference program's by a relative error of at most 0.022.
Values may be sent and summed in bfloat16 or wider, within the bound.
No kernel may reach another device: no remote copies, remote signals or barrier semaphores. Data moves between devices by JAX's collectives and lax.ppermute only.
A program may use at most 192 MiB of HBM per device.

```python
import math
import jax
import jax.numpy as jnp
from jax import lax

D = 2048
QH = 32
KVH = 8
HD = 64
FF = 8192
LEN = 1024
TOKENS = 8192
N_TENSOR = 4


def document_layout(key):
    sequences = TOKENS // LEN
    level_key = jax.random.fold_in(key, 11)
    start_key = jax.random.fold_in(key, 12)
    rate_level = jax.random.randint(level_key, (sequences, 1), 0, 5)
    spacing = jnp.left_shift(jnp.int32(4), 2 * rate_level)
    coin_flips = jax.random.randint(start_key, (sequences, LEN), 0, spacing)
    place_index = jnp.arange(LEN, dtype=jnp.int32)[None, :]
    sequence_index = jnp.arange(sequences, dtype=jnp.int32)[:, None]
    boundary = (coin_flips == 0) & (place_index > 0) & (sequence_index > 0)
    last_start = (sequence_index == sequences - 1) & (place_index == LEN - 1)
    boundary = boundary | last_start
    doc_start = lax.cummax(jnp.where(boundary, place_index, 0), axis=1)
    within_doc = place_index - doc_start
    return (doc_start.reshape(-1).astype(jnp.int32), within_doc.reshape(-1).astype(jnp.int32))


def draw_segments(key, part):
    return document_layout(key)[0]


def draw_positions(key, part):
    return document_layout(key)[1]


def levels(rng, extent, pieces, smallest, top_value):
    gain, own = 1.0, jax.random.fold_in(rng, 6)
    for axis_at, blocks in pieces:
        steps = jnp.exp(jax.random.uniform(jax.random.fold_in(own, axis_at), (blocks,), jnp.float32, smallest / len(pieces), top_value / len(pieces)))
        gain = gain * jnp.repeat(steps, extent[axis_at] // blocks).reshape([-1 if axis == axis_at else 1 for axis in range(len(extent))])
    return gain


def normal_values(stream_key, dims, spread, bound, shards=(), kind=jnp.bfloat16):
    drawn = jax.random.normal(stream_key, dims, jnp.float32) * spread
    if len(shards) > 0:
        drawn = levels(stream_key, dims, shards, -0.22, 0.18) * drawn
    return jnp.clip(drawn, min=-bound, max=bound).astype(kind)


def setup_inputs(seed: int = 0) -> dict:
    splits = jax.random.split(jax.random.key(seed), 14)
    return {
        "tokens": normal_values(splits[0], (TOKENS, D), 1.0, 6.0, ((0, 32),)),
        "segments": draw_segments(jax.random.fold_in(splits[13], 71), 0),
        "positions": draw_positions(jax.random.fold_in(splits[13], 71), 0),
        "norm_attn": jnp.clip(1.0 + 0.15 * jax.random.normal(splits[3], (D,), jnp.float32), 0.25, 1.75),
        "w_query": normal_values(splits[4], (D, QH * HD), D ** -0.5, 0.125, ((0, 8), (1, 4))),
        "w_key": normal_values(splits[5], (D, KVH * HD), D ** -0.5, 0.125, ((0, 8), (1, 4))),
        "w_value": normal_values(splits[6], (D, KVH * HD), D ** -0.5, 0.125, ((0, 8), (1, 4))),
        "w_out": normal_values(splits[7], (QH * HD, D), (QH * HD // 8) ** -0.5, 0.375, ((0, 4), (1, 8))),
        "norm_mlp": jnp.clip(1.0 + 0.15 * jax.random.normal(splits[8], (D,), jnp.float32), 0.25, 1.75),
        "w_gate": normal_values(splits[9], (D, FF), D ** -0.5, 0.125, ((0, 8), (1, 4))),
        "w_up": normal_values(splits[10], (D, FF), D ** -0.5, 0.125, ((0, 8), (1, 4))),
        "w_down": normal_values(splits[11], (FF, D), (FF // 2) ** -0.5, 0.09375, ((0, 4), (1, 8))),
        "cotangent": normal_values(splits[12], (TOKENS, D), 1.0, 6.0, ((0, 32),)),
    }


@jax.custom_vjp
def low(v):
    return lax.optimization_barrier(v.astype(jnp.bfloat16)).astype(jnp.float32)

@jax.custom_vjp
def low_back(v):
    return v

def low_keep(v):
    return (low(v), None)

def low_pass(kept, grad):
    return (grad,)

def back_keep(v):
    return (v, None)

def back_low(kept, grad):
    return (low(grad),)
low.defvjp(low_keep, low_pass)
low_back.defvjp(back_keep, back_low)
highest = lax.Precision.HIGHEST

def matmul_high(left_side, right_side):
    return jnp.dot(left_side, right_side, precision=highest, preferred_element_type=jnp.float32)

def rms_scale(values, norm_gain):
    inverse = lax.rsqrt(lax.optimization_barrier(jnp.mean(values * values, axis=-1, keepdims=True)) + 1e-05)
    return values * inverse * norm_gain

def rotary_tables(positions):
    freq_index = jnp.arange(HD // 2, dtype=jnp.int32).astype(jnp.float32)
    inverse = jnp.exp(freq_index * (-2.0 * math.log(500000.0) / HD))
    angles = positions.astype(jnp.float32)[:, None] * inverse[None, :]
    return (jnp.cos(angles), jnp.sin(angles))

def rotate(values, cosine_table, sine_table):
    half_width = values.shape[-1] // 2
    lower_half = values[..., :half_width]
    upper_half = values[..., half_width:]
    cosine_rows = cosine_table[:, None, :]
    sine_rows = sine_table[:, None, :]
    return jnp.concatenate([lower_half * cosine_rows - upper_half * sine_rows, upper_half * cosine_rows + lower_half * sine_rows], axis=-1)

def split_product(left_side, right_side):
    part_width = left_side.shape[1] // N_TENSOR
    left_parts = left_side.reshape(left_side.shape[0], N_TENSOR, part_width)
    right_parts = right_side.reshape(N_TENSOR, part_width, right_side.shape[1])
    group_terms = jnp.einsum('rgw,gwd->grd', left_parts, right_parts, precision=highest)
    return lax.optimization_barrier(jnp.sum(low(group_terms), axis=0))

def attend_sequence(all_queries, all_keys, all_values, segment_ids):
    block_rows = min(512, LEN)
    score_scale = 1.0 / math.sqrt(HD)
    place_index = jnp.arange(LEN, dtype=jnp.int32)

    def one_block(block_index):
        row_start = block_index * block_rows
        query_rows = lax.dynamic_slice_in_dim(all_queries, row_start, block_rows, 0)
        query_segs = lax.dynamic_slice_in_dim(segment_ids, row_start, block_rows, 0)
        query_place = row_start + jnp.arange(block_rows, dtype=jnp.int32)
        scores = jnp.einsum('qhgd,khd->hgqk', query_rows, all_keys, precision=highest) * score_scale
        scores = low_back(scores)
        allowed = (place_index[None, :] <= query_place[:, None]) & (segment_ids[None, :] == query_segs[:, None])
        scores = jnp.where(allowed, scores, -1e+30)
        attn_probs = jax.nn.softmax(scores, axis=-1)
        return jnp.einsum('hgqk,khd->qhgd', low(attn_probs), all_values, precision=highest)
    blocks = lax.map(jax.checkpoint(one_block), jnp.arange(LEN // block_rows, dtype=jnp.int32))
    return blocks.reshape(LEN, QH * HD)

def layer_rows(params, token_rows, segment_ids, positions):
    norm_attn, w_query, w_key, w_value, w_out, norm_mlp, w_gate, w_up, w_down = params
    row_count = token_rows.shape[0]
    sequences = row_count // LEN
    normed_in = low(rms_scale(token_rows, norm_attn))
    cosine_table, sine_table = rotary_tables(positions)
    query_raw = low_back(matmul_high(normed_in, w_query).reshape(row_count, QH, HD))
    key_raw = low_back(matmul_high(normed_in, w_key).reshape(row_count, KVH, HD))
    all_queries = low(rotate(query_raw, cosine_table, sine_table)).reshape(sequences, LEN, KVH, QH // KVH, HD)
    all_keys = low(rotate(key_raw, cosine_table, sine_table)).reshape(sequences, LEN, KVH, HD)
    all_values = low_back(low(matmul_high(normed_in, w_value))).reshape(sequences, LEN, KVH, HD)
    seq_segments = segment_ids.reshape(sequences, LEN)

    def one_sequence(seq_inputs):
        return attend_sequence(seq_inputs[0], seq_inputs[1], seq_inputs[2], seq_inputs[3])
    context = lax.map(one_sequence, (all_queries, all_keys, all_values, seq_segments))
    context = low_back(low(context.reshape(row_count, QH * HD)))
    attn_branch = low_back(split_product(context, w_out))
    middle = token_rows + attn_branch
    normed_mid = low(rms_scale(middle, norm_mlp))
    gate_values = low_back(matmul_high(normed_mid, w_gate))
    up_values = low_back(matmul_high(normed_mid, w_up))
    hidden = low(jax.nn.silu(gate_values) * up_values)
    mlp_branch = low_back(split_product(hidden, w_down))
    return middle + mlp_branch

def reference(tokens, segments, positions, norm_attn, w_query, w_key, w_value, w_out, norm_mlp, w_gate, w_up, w_down, cotangent):
    seq_total = TOKENS // LEN
    group_seqs = math.gcd(seq_total, max(1, 4096 // LEN))
    group_count = seq_total // group_seqs
    group_rows = group_seqs * LEN
    seg_groups = segments.reshape(group_count, group_rows)
    pos_groups = positions.reshape(group_count, group_rows)

    def forward(token_values, attn_gain, query_weight, key_weight, value_weight, out_weight, mlp_gain, gate_weight, up_weight, down_weight):
        params = (attn_gain, query_weight, key_weight, value_weight, out_weight, mlp_gain, gate_weight, up_weight, down_weight)

        def one_group(group_inputs):
            return layer_rows(params, group_inputs[0], group_inputs[1], group_inputs[2])
        outputs = lax.map(jax.checkpoint(one_group), (token_values.reshape(group_count, group_rows, D), seg_groups, pos_groups))
        return outputs.reshape(TOKENS, D)
    layer_out, pullback = jax.vjp(forward, tokens.astype(jnp.float32), norm_attn.astype(jnp.float32), w_query.astype(jnp.float32), w_key.astype(jnp.float32), w_value.astype(jnp.float32), w_out.astype(jnp.float32), norm_mlp.astype(jnp.float32), w_gate.astype(jnp.float32), w_up.astype(jnp.float32), w_down.astype(jnp.float32))
    gradients = pullback(cotangent.astype(jnp.float32))
    return (layer_out.astype(jnp.bfloat16), gradients[0], gradients[1], gradients[2], gradients[3], gradients[4], gradients[5], gradients[6], gradients[7], gradients[8], gradients[9])
```

```python
from functools import partial
import math

import jax
import jax.numpy as jnp
from jax import lax
from jax.experimental import pallas as pl
from jax.experimental.pallas import tpu as pltpu
from jax.sharding import PartitionSpec as P


QH = 32
KVH = 8
HD = 64
LEN = 1024
WIDTH = 2048
GROUP = QH // KVH
LANES = 128
TILE = 256
NEG = -1e30
DP, TENSOR = "dp", "tensor"
EPS = 1e-05
VMEM_LIMIT = 58 << 20


f32 = jnp.float32
bf16 = jnp.bfloat16


def dot(a, b, contract):
    return lax.dot_general(a, b, (contract, ((), ())), preferred_element_type=f32)


def ways_of(n):
    return 2 if WIDTH // n >= 2 * LANES else 1


def routes_of(n):
    bits = list(range(1, n.bit_length() - 1))
    return [bits, bits[::-1]][: ways_of(n)]


def block_slots(n):
    count, ways = n // 2, ways_of(n)
    return [(h, 0) for h in range(ways)] + [(h, s) for h in range(ways) for s in range(1, count)]


def width_order(n):
    routes, ways = routes_of(n), ways_of(n)
    order = []
    for core in range(2):
        for h, s in block_slots(n):
            j = core
            for t, b in enumerate(routes[h]):
                j |= ((s >> t) & 1) << b
            order.append(ways * j + h)
    return order


def swap(x, axis, n, b):
    return lax.ppermute(x, axis, [(i, i ^ (1 << b)) for i in range(n)])


def dp_gather(shard, n):
    routes, ways = routes_of(n), ways_of(n)
    size = shard.shape[0] // ways
    parts = [[shard[h * size : (h + 1) * size]] for h in range(ways)]
    for t in range(len(routes[0])):
        for h in range(ways):
            parts[h] += [swap(p, DP, n, routes[h][t]) for p in parts[h]]
    own = [shard] + [p for part in parts for p in part[1:]]
    return own + [swap(p, DP, n, 0) for p in own]


def scatter_segments(n):
    count, ways = n // 2, ways_of(n)
    size = WIDTH // n // ways
    half = count // 2
    cuts = [(ways + half - 1) * size, half * size]
    if ways > 1:
        cuts += [(half - 1) * size, half * size]
    return size, cuts


def add_kernel(*refs, spans):
    count = len(spans)
    for i, (at, rows, size) in enumerate(spans):
        kept, got, out = refs[2 * i], refs[2 * i + 1], refs[2 * count + i]
        total = kept[pl.ds(at, rows), :].astype(f32) + got[pl.ds(size, rows), :].astype(f32)
        out[...] = total.astype(bf16)


def add_rows(pairs, size):
    tile = 1024
    columns = pairs[0][0].shape[1]
    arrays = [x for array, _, _, got in pairs for x in (array, got)]
    return pl.pallas_call(
        partial(add_kernel, spans=[(at, rows, size) for _, at, rows, _ in pairs]),
        grid=(columns // tile,),
        in_specs=[pl.BlockSpec((x.shape[0], tile), lambda i: (0, i)) for x in arrays],
        out_specs=tuple(pl.BlockSpec((rows, tile), lambda i: (0, i)) for _, _, rows, _ in pairs),
        out_shape=tuple(jax.ShapeDtypeStruct((rows, columns), bf16) for _, _, rows, _ in pairs),
        compiler_params=pltpu.CompilerParams(vmem_limit_bytes=VMEM_LIMIT),
    )(*arrays)


def dp_scatter(pieces, n):
    routes, ways = routes_of(n), ways_of(n)
    size, _ = scatter_segments(n)
    kept = [(pieces[0], ways * size)] + ([(pieces[2], 0)] if ways > 1 else [])
    send = [pieces[1]] + ([pieces[3]] if ways > 1 else [])
    terms = [[] for _ in range(ways)]
    slots = n // 4
    for t in reversed(range(len(routes[0]))):
        for h in range(ways):
            terms[h].append(swap(send[h], DP, n, routes[h][t]))
        if t:
            rows = (slots - 1) * size
            sums = add_rows([(*kept[h], rows, terms[h][-1]) for h in range(ways)], size)
            slots //= 2
            send = [x[(slots - 1) * size :] if slots > 1 else x for x in sums]
            kept = [(x, 0) for x in sums]
    return pieces[0], terms


def width_at(order_ref, k, width):
    return pl.ds(pl.multiple_of(order_ref[k] * width, width), width)


def reorder_kernel(order_ref, *refs, inverse):
    ins, outs = refs[: len(refs) // 2], refs[len(refs) // 2 :]
    count = order_ref.shape[0]
    for src, dst in zip(ins, outs):
        width = src.shape[1] // count
        for k in range(count):
            here = pl.ds(k * width, width)
            if inverse:
                dst[:, width_at(order_ref, k, width)] = src[:, here]
            else:
                dst[:, here] = src[:, width_at(order_ref, k, width)]


SMEM_SPEC = pl.BlockSpec(memory_space=pltpu.SMEM)
VMEM_SPEC = pl.BlockSpec(memory_space=pltpu.VMEM)


def reorder(order, arrays, inverse):
    return pl.pallas_call(
        partial(reorder_kernel, inverse=inverse),
        out_shape=tuple(jax.ShapeDtypeStruct(a.shape, a.dtype) for a in arrays),
        in_specs=[SMEM_SPEC] + [VMEM_SPEC] * len(arrays),
        out_specs=tuple(VMEM_SPEC for _ in arrays),
    )(order, *arrays)


def unpack_kernel(me_ref, *refs, kv):
    out_ref = refs[-1]
    count = len(refs) - 1
    for s, ref in enumerate(refs[:-1]):
        z = jnp.bitwise_xor(me_ref[0], s)
        for i in range(2):
            at = pl.ds(pl.multiple_of((i * count + z) * kv, kv), kv)
            out_ref[:, at] = ref[:, pl.ds(i * kv, kv)]


def unpack_kv(me, slots, kv):
    rows = slots[0].shape[0]
    return pl.pallas_call(
        partial(unpack_kernel, kv=kv),
        out_shape=jax.ShapeDtypeStruct((rows, 2 * kv * len(slots)), bf16),
        in_specs=[SMEM_SPEC] + [VMEM_SPEC] * len(slots),
        out_specs=VMEM_SPEC,
        name="uk",
    )(me, *slots)


def unpack_pair_kernel(in_ref, *outs):
    rows, width = outs[0].shape[0], in_ref.shape[1] // len(outs)
    for z in range(in_ref.shape[0] // rows):
        for i, out in enumerate(outs):
            out[:, pl.ds(z * width, width)] = in_ref[pl.ds(z * rows, rows), pl.ds(i * width, width)]


def unpack_pair(x, n_tensor):
    rows, total = x.shape[0] // n_tensor, x.shape[1] * n_tensor // 2
    return pl.pallas_call(
        unpack_pair_kernel,
        out_shape=tuple(jax.ShapeDtypeStruct((rows, total), x.dtype) for _ in range(2)),
        in_specs=[VMEM_SPEC],
        out_specs=(VMEM_SPEC, VMEM_SPEC),
        name="uq",
    )(x)


def shard_sum(first_ref, terms, ways, at):
    parts = []
    for h in range(ways):
        size = terms[h][-1].shape[0]
        total = first_ref[pl.ds(h * size, size), at].astype(f32)
        for t in terms[h]:
            total = total + t[pl.ds(0, size), at].astype(f32)
        parts.append(total)
    return parts[0] if ways == 1 else jnp.concatenate(parts, axis=0)


def split_terms(refs, ways):
    each = len(refs) // ways
    return [refs[h * each : (h + 1) * each] for h in range(ways)]


def flat(scattered):
    first, terms = scattered
    return [first] + [t for part in terms for t in part]


def pack_kernel(*refs, n_tensor, ways, groups):
    out_ref = refs[-1]
    rows = out_ref.shape[0] // n_tensor
    count = (len(refs) - 1) // len(groups)
    for i, cuts in enumerate(groups):
        mine = refs[i * count : (i + 1) * count]
        terms = split_terms(mine[1:], ways)
        for z in range(n_tensor):
            for at, width, start in cuts:
                total = shard_sum(mine[0], terms, ways, pl.ds(start + z * width, width))
                out_ref[pl.ds(z * rows, rows), pl.ds(at, width)] = total.astype(out_ref.dtype)


def pack(scattered, groups, n_tensor, ways, columns, rows):
    arrays = [a for s in scattered for a in flat(s)]
    return pl.pallas_call(
        partial(pack_kernel, n_tensor=n_tensor, ways=ways, groups=groups),
        out_shape=jax.ShapeDtypeStruct((n_tensor * rows, columns), bf16),
        in_specs=[VMEM_SPEC] * len(arrays),
        out_specs=VMEM_SPEC,
        compiler_params=pltpu.CompilerParams(vmem_limit_bytes=VMEM_LIMIT),
    )(*arrays)


def final_kernel(*refs, ways, transposed):
    out_ref = refs[-1]
    total = shard_sum(refs[0], split_terms(refs[1:-1], ways), ways, slice(None))
    out_ref[...] = total.T if transposed else total


def finish(scattered, start, columns, ways, transposed):
    arrays = flat(scattered)
    size = scattered[1][0][-1].shape[0]
    rows = ways * size
    tile = 512
    base = start // tile
    blocks = [rows] + [size] * (len(arrays) - 1)
    return pl.pallas_call(
        partial(final_kernel, ways=ways, transposed=transposed),
        grid=(columns // tile,),
        out_shape=jax.ShapeDtypeStruct((columns, rows) if transposed else (rows, columns), f32),
        in_specs=[pl.BlockSpec((b, tile), lambda i: (0, base + i)) for b in blocks],
        out_specs=pl.BlockSpec((tile, rows) if transposed else (rows, tile), (lambda i: (i, 0)) if transposed else (lambda i: (0, i))),
    )(*arrays)


def joined(refs):
    return jnp.concatenate([r[...] for r in refs], axis=0)


def piece_specs(pieces, tile, column):
    return [pl.BlockSpec((p.shape[0], tile), lambda i, *_: (0, column(i))) for p in pieces]


def swap_halves(u):
    lane = lax.broadcasted_iota(jnp.int32, u.shape, 1)
    up = pltpu.roll(u, HD // 2, 1)
    down = pltpu.roll(u, LANES - HD // 2, 1)
    return jnp.where((lane % HD) < HD // 2, down, up)


def turn(u, cosine, signed_sine, back):
    s = swap_halves(u) * signed_sine
    return u * cosine - s if back else u * cosine + s


def proj_kv_kernel(x_ref, cos_ref, sin_ref, *refs, key_tiles):
    out_ref = refs[-1]
    raw = dot(x_ref[...], joined(refs[:-1]), ((1,), (0,)))
    is_key = pl.program_id(0) < key_tiles
    cosine = jnp.where(is_key, cos_ref[...], 1.0)
    sine = jnp.where(is_key, sin_ref[...], 0.0)
    for c in range(raw.shape[1] // LANES):
        part = raw[:, c * LANES : (c + 1) * LANES]
        out_ref[:, pl.ds(c * LANES, LANES)] = turn(part, cosine, sine, False).astype(bf16)


def proj_kv(x, cosine, sine, pieces):
    rows = x.shape[0]
    whole = lambda shape: pl.BlockSpec(shape, lambda i: (0, 0))
    return pl.pallas_call(
        partial(proj_kv_kernel, key_tiles=KVH * HD // TILE),
        grid=(2 * KVH * HD // TILE,),
        in_specs=[whole(x.shape), whole(cosine.shape), whole(sine.shape)] + piece_specs(pieces, TILE, lambda i: i),
        out_specs=pl.BlockSpec((rows, TILE), lambda i: (0, i)),
        out_shape=jax.ShapeDtypeStruct((rows, 2 * KVH * HD), bf16),
        cost_estimate=pl.CostEstimate(flops=4 * rows * WIDTH * KVH * HD, bytes_accessed=6 << 20, transcendentals=0),
        compiler_params=pltpu.CompilerParams(vmem_limit_bytes=VMEM_LIMIT),
        name="pk",
    )(x, cosine, sine, *pieces)


def rope_kv_kernel(kv_ref, cos_ref, sin_ref, out_ref, *, key_width):
    cosine, sine = cos_ref[...], sin_ref[...]
    for c in range(key_width // LANES):
        at = pl.ds(c * LANES, LANES)
        out_ref[:, at] = turn(kv_ref[:, at].astype(f32), cosine, sine, True).astype(bf16)
    out_ref[:, key_width:] = kv_ref[:, key_width:]


def rope_kv_back(kv, cosine, sine):
    return pl.pallas_call(
        partial(rope_kv_kernel, key_width=kv.shape[1] // 2),
        out_shape=jax.ShapeDtypeStruct(kv.shape, bf16),
        name="rk",
    )(kv, cosine, sine)


def split_halves(block, odd):
    wide = block.astype(f32)
    rolled = pltpu.roll(wide, HD, 1)
    lane = lax.broadcasted_iota(jnp.int32, wide.shape, 1)
    low = lane < HD
    first = jnp.where(odd, rolled, wide)
    second = jnp.where(odd, wide, rolled)
    zero = jnp.zeros_like(wide)
    return jnp.where(low, first, zero).astype(bf16), jnp.where(low, zero, second).astype(bf16)


def attn_fwd_kernel(row0_ref, seg_ref, x_ref, k_ref, v_ref, cos_ref, sin_ref, *refs, count):
    w_query = refs[:count]
    ctx_ref, rot_ref, lse_ref, bias_ref = refs[-4:]
    g = pl.program_id(0)
    rows = x_ref.shape[0]

    @pl.when(g == 0)
    def _():
        t = row0_ref[0] + lax.broadcasted_iota(jnp.int32, bias_ref.shape, 0)
        s = lax.broadcasted_iota(jnp.int32, bias_ref.shape, 1)
        allowed = (s <= t) & (s >= seg_ref[...])
        bias_ref[...] = jnp.where(allowed, 0.0, NEG)

    q_raw = dot(x_ref[...], joined(w_query), ((1,), (0,)))
    odd = lax.rem(g, 2) == 1
    keys = split_halves(k_ref[...], odd)
    values = split_halves(v_ref[...], odd)
    lane = lax.broadcasted_iota(jnp.int32, (rows, LANES), 1)
    log_sums = jnp.zeros((rows, LANES), f32)
    for c in range(GROUP // 2):
        at = pl.ds(c * LANES, LANES)
        turned = turn(q_raw[:, c * LANES : (c + 1) * LANES], cos_ref[...], sin_ref[...], False)
        query = (turned * (HD**-0.5)).astype(bf16)
        rot_ref[:, at] = query
        total = jnp.zeros((rows, LANES), f32)
        for e in range(2):
            scores = dot(query, keys[e], ((1,), (1,))) + bias_ref[...]
            peak = jnp.max(scores, axis=1, keepdims=True)
            weights = jnp.exp(scores - peak)
            mass = jnp.sum(weights, axis=1, keepdims=True)
            part = dot(weights.astype(bf16), values[e], ((1,), (0,)))
            total = total + part * (1.0 / mass)
            log_sums = jnp.where(lane == 2 * c + e, peak + jnp.log(mass), log_sums)
        ctx_ref[:, at] = total.astype(bf16)
    lse_ref[...] = log_sums


FWD_PARTS = 2


def attn_forward(row0, seg_col, x, kv, cosine, sine, pieces, part, before):
    rows = x.shape[0]
    half = KVH * HD // LANES
    heads = KVH // FWD_PARTS
    base = part * heads
    args = [row0, seg_col, x, kv, kv, cosine, sine, *pieces]
    whole = lambda shape: pl.BlockSpec(shape, lambda g, r: (0, 0))
    grid_spec = pltpu.PrefetchScalarGridSpec(
        num_scalar_prefetch=1,
        grid=(heads,),
        in_specs=[
            whole((rows, 1)),
            whole(x.shape),
            pl.BlockSpec((LEN, LANES), lambda g, r: (0, (base + g) // 2)),
            pl.BlockSpec((LEN, LANES), lambda g, r: (0, half + (base + g) // 2)),
            whole((rows, LANES)),
            whole((rows, LANES)),
        ]
        + piece_specs(pieces, TILE, lambda g: base + g)
        + [pl.BlockSpec(memory_space=pl.ANY)] * len(before),
        out_specs=[
            pl.BlockSpec((rows, TILE), lambda g, r: (0, base + g)),
            pl.BlockSpec((rows, TILE), lambda g, r: (0, base + g)),
            pl.BlockSpec((rows, LANES), lambda g, r: (0, base + g)),
        ],
        scratch_shapes=[pltpu.VMEM((rows, LEN), f32)],
    )
    return pl.pallas_call(
        partial(attn_fwd_kernel, count=len(pieces)),
        grid_spec=grid_spec,
        out_shape=(
            jax.ShapeDtypeStruct((rows, QH * HD), bf16),
            jax.ShapeDtypeStruct((rows, QH * HD), bf16),
            jax.ShapeDtypeStruct((rows, KVH * LANES), f32),
        ),
        cost_estimate=pl.CostEstimate(
            flops=8 * rows * LEN * QH * HD, bytes_accessed=12 << 20, transcendentals=rows * LEN * QH // FWD_PARTS
        ),
        compiler_params=pltpu.CompilerParams(vmem_limit_bytes=VMEM_LIMIT),
        input_output_aliases={len(args) + i: i for i in range(len(before))},
    )(*args, *before)


def out_proj_kernel(ctx_ref, tok_ref, gain_ref, *refs):
    mid_ref, norm_ref, sum_ref = refs[-3:]
    i = pl.program_id(0)

    @pl.when(i == 0)
    def _():
        sum_ref[...] = tok_ref[...].astype(f32)

    sum_ref[...] += dot(ctx_ref[...], joined(refs[:-3]), ((1,), (1,)))

    @pl.when(i == pl.num_programs(0) - 1)
    def _():
        middle = sum_ref[...]
        mid_ref[...] = middle
        inverse = lax.rsqrt(jnp.mean(middle * middle, axis=1, keepdims=True) + EPS)
        norm_ref[...] = (middle * inverse * gain_ref[...]).astype(bf16)


def out_proj(context, tokens, gain, pieces):
    rows = context.shape[0]
    tile = 512
    whole = lambda shape: pl.BlockSpec(shape, lambda i: (0, 0))
    return pl.pallas_call(
        out_proj_kernel,
        grid=(QH * HD // tile,),
        in_specs=[pl.BlockSpec((rows, tile), lambda i: (0, i)), whole(tokens.shape), whole(gain.shape)]
        + piece_specs(pieces, tile, lambda i: i),
        out_specs=(whole((rows, WIDTH)), whole((rows, WIDTH))),
        out_shape=(jax.ShapeDtypeStruct((rows, WIDTH), f32), jax.ShapeDtypeStruct((rows, WIDTH), bf16)),
        scratch_shapes=[pltpu.VMEM((rows, WIDTH), f32)],
        cost_estimate=pl.CostEstimate(flops=2 * rows * WIDTH * QH * HD, bytes_accessed=14 << 20, transcendentals=0),
        compiler_params=pltpu.CompilerParams(vmem_limit_bytes=VMEM_LIMIT),
        name="op",
    )(context, tokens, gain, *pieces)


def rms_back(values, gain, grad):
    inverse = lax.rsqrt(jnp.mean(values * values, axis=1, keepdims=True) + EPS)
    scaled = gain * grad
    along = jnp.mean(scaled * values, axis=1, keepdims=True)
    d_values = inverse * scaled - values * (inverse * inverse * inverse) * along
    d_gain = jnp.sum(grad * values * inverse, axis=0, keepdims=True)
    return d_values, d_gain


def mid_back_kernel(mid_ref, gain_ref, cot_ref, *refs):
    dmid_ref, db_ref, dg_ref = refs[-3:]
    d_values, d_gain = rms_back(mid_ref[...], gain_ref[...], joined(refs[:-3]).astype(f32))
    d_middle = cot_ref[...].astype(f32) + d_values
    dmid_ref[...] = d_middle
    db_ref[...] = d_middle.astype(bf16)
    dg_ref[...] = jnp.broadcast_to(d_gain, dg_ref.shape)


def mid_back(d_normed, middle, gain, cot):
    rows = middle.shape[0]
    return pl.pallas_call(
        mid_back_kernel,
        out_shape=(
            jax.ShapeDtypeStruct((rows, WIDTH), f32),
            jax.ShapeDtypeStruct((rows, WIDTH), bf16),
            jax.ShapeDtypeStruct((8, WIDTH), f32),
        ),
        name="mb",
    )(middle, gain, cot, *d_normed)


def attn_bwd_kernel(
    row0_ref, seg_ref, q_ref, k_ref, v_ref, db_ref, ctx_ref, lse_ref, cos_ref, sin_ref, *refs, count
):
    w_query, w_out = refs[:count], refs[count : 2 * count]
    dq_ref, dk_ref, dv_ref, dn_ref, bias_ref = refs[2 * count :]
    g = pl.program_id(0)
    rows = q_ref.shape[0]

    @pl.when(g == 0)
    def _():
        s = lax.broadcasted_iota(jnp.int32, bias_ref.shape, 0)
        t = row0_ref[0] + lax.broadcasted_iota(jnp.int32, bias_ref.shape, 1)
        allowed = (s <= t) & (s >= seg_ref[...])
        bias_ref[...] = jnp.where(allowed, 0.0, NEG)
        dn_ref[...] = jnp.zeros_like(dn_ref)

    d_context = dot(db_ref[...], joined(w_out), ((1,), (0,))).astype(bf16)
    odd = lax.rem(g, 2) == 1
    keys = split_halves(k_ref[...], odd)
    values = split_halves(v_ref[...], odd)
    log_sums = lse_ref[...].T
    low = lax.broadcasted_iota(jnp.int32, (rows, LANES), 1) < HD
    dk_sum = jnp.zeros((LEN, LANES), f32)
    dv_sum = jnp.zeros((LEN, LANES), f32)
    for c in range(GROUP // 2):
        at = pl.ds(c * LANES, LANES)
        query, d_rows = q_ref[:, at], d_context[:, c * LANES : (c + 1) * LANES]
        both = (d_rows.astype(f32) * ctx_ref[:, at].astype(f32)).T
        dq = jnp.zeros((rows, LANES), f32)
        for e in range(2):
            mine = low if e == 0 else jnp.logical_not(low)
            delta = jnp.sum(both[e * HD : (e + 1) * HD], axis=0, keepdims=True)
            h = 2 * c + e
            scores = dot(keys[e], query, ((1,), (1,))) + bias_ref[...]
            probs = jnp.exp(scores - log_sums[h : h + 1])
            d_probs = dot(values[e], d_rows, ((1,), (1,)))
            d_scores = (probs * (d_probs - delta)).astype(bf16)
            zero = jnp.zeros_like(query)
            dv_sum = dv_sum + dot(probs.astype(bf16), jnp.where(mine, d_rows, zero), ((1,), (0,)))
            dk_sum = dk_sum + dot(d_scores, jnp.where(mine, query, zero), ((1,), (0,)))
            dq = dq + dot(d_scores, keys[e], ((0,), (0,)))
        dq_ref[:, at] = turn(dq * (HD**-0.5), cos_ref[...], sin_ref[...], True).astype(bf16)
    dn_ref[...] += dot(dq_ref[...], joined(w_query), ((1,), (1,)))
    wide_low = lax.broadcasted_iota(jnp.int32, (LEN, LANES), 1) < HD
    keep = wide_low == odd
    for total, out in ((dk_sum, dk_ref), (dv_sum, dv_ref)):
        folded = (total + pltpu.roll(total, HD, 1)).astype(bf16)
        out[...] = jnp.where(keep, out[...], folded)


def attn_backward(row0, seg_row, query, kv, d_branch, context, lse, cosine, sine, q_pieces, out_pieces):
    rows = query.shape[0]
    half = KVH * HD // LANES
    whole = lambda shape: pl.BlockSpec(shape, lambda g, r: (0, 0))
    grid_spec = pltpu.PrefetchScalarGridSpec(
        num_scalar_prefetch=1,
        grid=(KVH,),
        in_specs=[
            whole((1, rows)),
            pl.BlockSpec((rows, TILE), lambda g, r: (0, g)),
            pl.BlockSpec((LEN, LANES), lambda g, r: (0, g // 2)),
            pl.BlockSpec((LEN, LANES), lambda g, r: (0, half + g // 2)),
            whole((rows, WIDTH)),
            pl.BlockSpec((rows, TILE), lambda g, r: (0, g)),
            pl.BlockSpec((rows, LANES), lambda g, r: (0, g)),
            whole((rows, LANES)),
            whole((rows, LANES)),
        ]
        + piece_specs(q_pieces, TILE, lambda g: g)
        + piece_specs(out_pieces, TILE, lambda g: g),
        out_specs=[
            pl.BlockSpec((rows, TILE), lambda g, r: (0, g)),
            pl.BlockSpec((LEN, LANES), lambda g, r: (0, g // 2)),
            pl.BlockSpec((LEN, LANES), lambda g, r: (0, g // 2)),
            whole((rows, WIDTH)),
        ],
        scratch_shapes=[pltpu.VMEM((LEN, rows), f32)],
    )
    return pl.pallas_call(
        partial(attn_bwd_kernel, count=len(q_pieces)),
        grid_spec=grid_spec,
        out_shape=(
            jax.ShapeDtypeStruct((rows, QH * HD), bf16),
            jax.ShapeDtypeStruct((LEN, KVH * HD), bf16),
            jax.ShapeDtypeStruct((LEN, KVH * HD), bf16),
            jax.ShapeDtypeStruct((rows, WIDTH), f32),
        ),
        cost_estimate=pl.CostEstimate(
            flops=28 * rows * LEN * QH * HD, bytes_accessed=28 << 20, transcendentals=rows * LEN * QH
        ),
        compiler_params=pltpu.CompilerParams(vmem_limit_bytes=VMEM_LIMIT),
        name="ab",
    )(row0, seg_row, query, kv, kv, d_branch, context, lse, cosine, sine, *q_pieces, *out_pieces)


def in_back_kernel(order_ref, dkv_ref, part_ref, tok_ref, gain_ref, dmid_ref, dg_mlp_ref, *refs):
    out_ref, dg_ref, sum_ref = refs[-3:]
    i = pl.program_id(0)

    @pl.when(i == 0)
    def _():
        sum_ref[...] = part_ref[...]
        dg_ref[...] = jnp.zeros_like(dg_ref)

    sum_ref[...] += dot(dkv_ref[...], joined(refs[:-3]), ((1,), (1,)))

    @pl.when(i == pl.num_programs(0) - 1)
    def _():
        d_values, d_gain = rms_back(tok_ref[...].astype(f32), gain_ref[...], sum_ref[...])
        d_values = d_values + dmid_ref[...]
        count = order_ref.shape[0]
        width = d_values.shape[1] // count
        for k in range(count):
            at = width_at(order_ref, k, width)
            out_ref[:, at] = d_values[:, k * width : (k + 1) * width]
            dg_ref[0:1, at] = d_gain[:, k * width : (k + 1) * width]
            dg_ref[1:2, at] = dg_mlp_ref[0:1, k * width : (k + 1) * width]


def in_back(order, d_kv, part, tokens, gain, d_middle, mlp_gain, pieces):
    rows = tokens.shape[0]
    whole = lambda shape: pl.BlockSpec(shape, lambda i: (0, 0))
    return pl.pallas_call(
        in_back_kernel,
        grid=(2 * KVH * HD // TILE,),
        in_specs=[SMEM_SPEC, pl.BlockSpec((rows, TILE), lambda i: (0, i))]
        + [whole(a.shape) for a in (part, tokens, gain, d_middle, mlp_gain)]
        + piece_specs(pieces, TILE, lambda i: i),
        out_specs=(whole((rows, WIDTH)), whole((8, WIDTH))),
        out_shape=(jax.ShapeDtypeStruct((rows, WIDTH), f32), jax.ShapeDtypeStruct((8, WIDTH), f32)),
        scratch_shapes=[pltpu.VMEM((rows, WIDTH), f32)],
        cost_estimate=pl.CostEstimate(flops=4 * rows * WIDTH * KVH * HD, bytes_accessed=16 << 20, transcendentals=0),
        compiler_params=pltpu.CompilerParams(vmem_limit_bytes=VMEM_LIMIT),
        name="ib",
    )(order, d_kv, part, tokens, gain, d_middle, mlp_gain, *pieces)


def mlp_kernel(me_ref, x_ref, *refs, slots, count):
    cots, refs = refs[: 2 * slots - 1], refs[2 * slots - 1 :]
    hidden_ref, grads_ref, cot_ref = refs[3 * count :]
    rows = cots[0].shape[0]

    @pl.when(pl.program_id(0) == 0)
    def _():
        for r in range(slots):
            z = lax.rem(me_ref[0] - r + slots, slots)
            value = cots[r][...] + cots[2 * slots - 1 - r][...] if r else cots[0][...]
            cot_ref[pl.ds(pl.multiple_of(z * rows, rows), rows), :] = value

    gate = dot(x_ref[...], joined(refs[:count]), ((1,), (0,)))
    up = dot(x_ref[...], joined(refs[count : 2 * count]), ((1,), (0,)))
    d_hidden = dot(cot_ref[...], joined(refs[2 * count : 3 * count]), ((1,), (0,)))
    sig = jax.nn.sigmoid(gate)
    silu = gate * sig
    hidden_ref[...] = (silu * up).astype(bf16)
    grads_ref[0] = (d_hidden * up * (sig + silu * (1.0 - sig))).astype(bf16)
    grads_ref[1] = (d_hidden * silu).astype(bf16)


def mlp(me, x, cots, chunk, pieces, down_pieces):
    rows = x.shape[0]
    slots = (len(cots) + 1) // 2
    ff = down_pieces[0].shape[1]
    tiles = ff // TILE
    whole = pl.BlockSpec((rows, WIDTH), lambda i: (0, 0))
    specs = [SMEM_SPEC, whole] + [pl.BlockSpec((rows // slots, WIDTH), lambda i: (chunk, 0))] * len(cots)
    for some, base in ((pieces, 0), (pieces, tiles), (down_pieces, 0)):
        specs += piece_specs(some, TILE, partial(lambda i, base: base + i, base=base))
    return pl.pallas_call(
        partial(mlp_kernel, slots=slots, count=len(pieces)),
        grid=(tiles,),
        in_specs=specs,
        out_specs=(
            pl.BlockSpec((rows, TILE), lambda i: (0, i)),
            pl.BlockSpec((2, rows, TILE), lambda i: (0, 0, i)),
            whole,
        ),
        out_shape=(
            jax.ShapeDtypeStruct((rows, ff), bf16),
            jax.ShapeDtypeStruct((2, rows, ff), bf16),
            jax.ShapeDtypeStruct((rows, WIDTH), bf16),
        ),
        cost_estimate=pl.CostEstimate(flops=6 * rows * WIDTH * ff, bytes_accessed=40 << 20, transcendentals=rows * ff),
        compiler_params=pltpu.CompilerParams(vmem_limit_bytes=VMEM_LIMIT),
    )(me, x, *cots, *pieces, *pieces, *down_pieces)


def back_kernel(x_ref, *refs):
    out_ref, sum_ref = refs[-2:]
    i = pl.program_id(0)
    part = dot(x_ref[...].reshape(x_ref.shape[-2:]), joined(refs[:-2]), ((1,), (1,)))

    @pl.when(i == 0)
    def _():
        sum_ref[...] = part

    @pl.when(i > 0)
    def _():
        sum_ref[...] += part

    @pl.when(i == pl.num_programs(0) - 1)
    def _():
        out_ref[...] = sum_ref[...].astype(bf16)


def back(x, pieces):
    many, rows, ff = x.shape
    tile = min(1024, ff)
    per = ff // tile
    return pl.pallas_call(
        back_kernel,
        grid=(many * per,),
        in_specs=[pl.BlockSpec((1, rows, tile), lambda i: (i // per, 0, i % per))]
        + piece_specs(pieces, tile, lambda i: i),
        out_specs=pl.BlockSpec((rows, WIDTH), lambda i: (0, 0)),
        out_shape=jax.ShapeDtypeStruct((rows, WIDTH), bf16),
        scratch_shapes=[pltpu.VMEM((rows, WIDTH), f32)],
        cost_estimate=pl.CostEstimate(flops=2 * many * rows * WIDTH * ff, bytes_accessed=(12 << 20) * many, transcendentals=0),
        compiler_params=pltpu.CompilerParams(vmem_limit_bytes=VMEM_LIMIT),
    )(x, *pieces)


def grad_kernel(*refs, chunks, received, cuts):
    lefts, rights = refs[:chunks], refs[chunks : 2 * chunks]
    outs, turned_ref = refs[2 * chunks + received : -1], refs[-1]

    @pl.when(pl.program_id(0) == 0)
    def _():
        depth = lefts[0].shape[0]
        for c, left in enumerate(lefts):
            turned_ref[:, pl.ds(c * depth, depth)] = left[...].T

    right = jnp.concatenate([r[...].reshape(r.shape[-2:]) for r in rights], axis=0)
    total = dot(turned_ref[...], right, ((1,), (0,)))
    if received:
        total = total + refs[2 * chunks][...].astype(f32)
    at = 0
    for out, rows in zip(outs, cuts):
        out[...] = total[at : at + rows].astype(bf16)
        at += rows


def weight_grad(lefts, rights, block, got, cuts):
    many, depth, columns = rights[0].shape
    rows = WIDTH // 2
    tile = min(512, columns)
    per = columns // tile
    chunks = len(lefts)
    column = lambda i: (0, i)
    extra = [got] if got is not None else []
    specs = [pl.BlockSpec((depth, rows), lambda i: (0, block))] * chunks
    specs += [pl.BlockSpec((1, depth, tile), lambda i: (i // per, 0, i % per))] * chunks
    specs += [pl.BlockSpec((rows, tile), column)] * len(extra)
    return pl.pallas_call(
        partial(grad_kernel, chunks=chunks, received=len(extra), cuts=cuts),
        grid=(many * per,),
        in_specs=specs,
        out_specs=tuple(pl.BlockSpec((c, tile), column) for c in cuts),
        out_shape=tuple(jax.ShapeDtypeStruct((c, many * columns), bf16) for c in cuts),
        scratch_shapes=[pltpu.VMEM((rows, depth * chunks), bf16)],
        cost_estimate=pl.CostEstimate(
            flops=2 * rows * depth * chunks * many * columns, bytes_accessed=8 * rows * many * columns, transcendentals=0
        ),
        compiler_params=pltpu.CompilerParams(vmem_limit_bytes=VMEM_LIMIT),
    )(*lefts, *rights, *extra)


def over_tensor(x, axis=0):
    return lax.all_gather(x, TENSOR, axis=axis, tiled=True)


def sum_tensor(x):
    return lax.psum_scatter(x, TENSOR, scatter_dimension=0, tiled=True)


def layer(
    tokens, segments, positions, norm_attn, w_query, w_key, w_value, w_out,
    norm_mlp, w_gate, w_up, w_down, cotangent, *, n_dp, n_tensor,
):
    me_dp, me_z = lax.axis_index(DP), lax.axis_index(TENSOR)
    rows, width = tokens.shape
    assert rows * n_tensor == LEN and width == WIDTH
    kv, q = w_key.shape[1], w_query.shape[1]
    ways = ways_of(n_dp)
    ff = w_gate.shape[1]
    order = jnp.bitwise_xor(jnp.array(width_order(n_dp), jnp.int32), ways * me_dp)
    row0 = (me_z * rows).reshape(1)
    own_positions = lax.dynamic_slice_in_dim(positions, me_z * rows, rows, 0)
    own_segs = lax.dynamic_slice_in_dim(segments, me_z * rows, rows, 0)

    if kv % LANES == 0:
        slots = [jnp.concatenate([w_key, w_value], axis=1)]
        for b in range(n_tensor.bit_length() - 1):
            slots += [swap(jnp.concatenate(slots, axis=0), TENSOR, n_tensor, b)]
            slots = [jnp.concatenate(slots, axis=0)]
        shard_rows = w_key.shape[0]
        slots = [slots[0][i * shard_rows : (i + 1) * shard_rows] for i in range(n_tensor)]
        kv_rows = unpack_kv(me_z.reshape(1), slots, kv)
    else:
        kv_rows = jnp.concatenate([over_tensor(w_key, 1), over_tensor(w_value, 1)], axis=1)
    kv_pieces = dp_gather(kv_rows, n_dp)
    q_rows, out_rows = unpack_pair(over_tensor(jnp.concatenate([w_query, w_out.T], axis=1)), n_tensor)
    q_pieces = dp_gather(q_rows, n_dp)
    out_pieces = dp_gather(out_rows, n_dp)
    gu_pieces = dp_gather(jnp.concatenate([w_gate, w_up], axis=1), n_dp)
    down_pieces = dp_gather(w_down.T, n_dp)

    gains = jnp.concatenate([norm_attn[None], norm_mlp[None], jnp.zeros((6, width), f32)], axis=0)
    tokens_here, cot_here, gains_here = reorder(order, (tokens, cotangent, gains), False)
    gain_attn, gain_mlp = gains_here[:1], gains_here[1:2]
    chunk = rows // 2
    chunks = [slice(i * chunk, (i + 1) * chunk) for i in range(2)]
    below, above = [cot_here], [cot_here]
    for r in range(1, n_tensor):
        below.append(lax.ppermute(below[-1], TENSOR, [(i, i + 1) for i in range(r - 1, n_tensor - 1)]))
        above.append(lax.ppermute(above[-1], TENSOR, [(i + 1, i) for i in range(n_tensor - r)]))
    cots = below + above[1:]

    freq_index = jnp.arange(HD // 2, dtype=jnp.int32).astype(f32)
    inverse = jnp.exp(freq_index * (-2.0 * math.log(500000.0) / HD))
    angles = own_positions.astype(f32)[:, None] * inverse[None, :]
    cosine = jnp.tile(jnp.cos(angles), (1, LANES // (HD // 2)))
    sine = jnp.sin(angles)
    sine = jnp.tile(jnp.concatenate([-sine, sine], axis=1), (1, LANES // HD))

    inputs = tokens_here.astype(f32)
    scale_in = lax.rsqrt(jnp.mean(inputs * inputs, axis=-1, keepdims=True) + EPS)
    normed_local = (inputs * scale_in * gain_attn).astype(bf16)
    kv_all = over_tensor(proj_kv(normed_local, cosine, sine, kv_pieces))
    attended = ()
    for i in range(FWD_PARTS):
        attended = attn_forward(row0, own_segs[:, None], normed_local, kv_all, cosine, sine, q_pieces, i, attended)
    context, query, lse = attended
    middle, normed_mid_local = out_proj(context, tokens_here, gain_mlp, out_pieces)
    normed_mid = [over_tensor(normed_mid_local[c]) for c in chunks]
    hidden, mlp_grads, cot_all, d_normed_mid, mlp_branch = [], [], [], [], []
    for i in range(2):
        h, g, c = mlp(me_z.reshape(1), normed_mid[i], cots, i, gu_pieces, down_pieces)
        cot_all.append(c)
        hidden.append(h[None])
        mlp_grads.append(g)
        d_normed_mid.append(sum_tensor(back(g, gu_pieces)))
        mlp_branch.append(sum_tensor(back(h[None], down_pieces)))
    _, cuts = scatter_segments(n_dp)
    half = [WIDTH // 2]

    def scattered(lefts, rights):
        other = weight_grad(lefts, rights, 1, None, half)[0]
        got = swap(other, DP, n_dp, 0)
        return dp_scatter(weight_grad(lefts, rights, 0, got, cuts), n_dp)

    down_parts = scattered(cot_all, hidden)
    gu_parts = scattered(normed_mid, mlp_grads)

    d_middle, d_branch, mlp_gain_part = mid_back(d_normed_mid, middle, gain_mlp, cot_here)
    dq, dk, dv, d_normed_part = attn_backward(
        row0, own_segs[None, :], query, kv_all, d_branch, context, lse, cosine, sine, q_pieces, out_pieces
    )
    out_parts = scattered([d_branch], [context[None]])
    d_kv = sum_tensor(jnp.concatenate([dk, dv], axis=1))
    query_parts = scattered([normed_local], [dq[None]])
    d_kv = rope_kv_back(d_kv, cosine, sine)
    kv_parts = scattered([normed_local], [d_kv[None]])
    input_grad, gain_parts = in_back(
        order, d_kv, d_normed_part, tokens_here, gain_attn, d_middle, mlp_gain_part, kv_pieces
    )

    grad_down = finish(down_parts, 0, ff, ways, True)
    grad_gate = finish(gu_parts, 0, ff, ways, False)
    grad_up = finish(gu_parts, ff, ff, ways, False)
    shard_rows = WIDTH // n_dp
    packed_qo = pack([query_parts, out_parts], [[(0, q, 0)], [(q, q, 0)]], n_tensor, ways, 2 * q, shard_rows)
    packed_qo = sum_tensor(packed_qo).astype(f32)
    grad_query, grad_output = packed_qo[:, :q], packed_qo[:, q:].T
    packed_kv = pack([kv_parts], [[(0, kv, 0), (kv, kv, kv * n_tensor)]], n_tensor, ways, 2 * kv, shard_rows)
    packed_kv = sum_tensor(packed_kv).astype(f32)
    grad_key, grad_value = packed_kv[:, :kv], packed_kv[:, kv:]

    def sum_all(x):
        for b in range(n_tensor.bit_length() - 1):
            x = x + swap(x, TENSOR, n_tensor, b)
        for b in range(n_dp.bit_length() - 1):
            x = x + swap(x, DP, n_dp, b)
        return x

    layer_out = (middle + jnp.concatenate(mlp_branch, axis=0).astype(f32)).astype(bf16)
    layer_out = reorder(order, (layer_out,), True)[0]
    gain_grads = sum_all(gain_parts)
    return (
        layer_out, input_grad, gain_grads[0], grad_query, grad_key, grad_value, grad_output,
        gain_grads[1], grad_gate, grad_up, grad_down,
    )


def solution(mesh):
    sizes = dict(mesh.shape)
    in_specs = (
        P((DP, TENSOR), None),
        P(DP),
        P(DP),
        P(),
        P(DP, TENSOR),
        P(DP, TENSOR),
        P(DP, TENSOR),
        P(TENSOR, DP),
        P(),
        P(DP, TENSOR),
        P(DP, TENSOR),
        P(TENSOR, DP),
        P((DP, TENSOR), None),
    )
    out_specs = (
        P((DP, TENSOR), None),
        P((DP, TENSOR), None),
        P(),
        P(DP, TENSOR),
        P(DP, TENSOR),
        P(DP, TENSOR),
        P(TENSOR, DP),
        P(),
        P(DP, TENSOR),
        P(DP, TENSOR),
        P(TENSOR, DP),
    )
    body = partial(layer, n_dp=sizes[DP], n_tensor=sizes[TENSOR])
    return jax.shard_map(body, mesh=mesh, in_specs=in_specs, out_specs=out_specs, check_vma=False)
```

```python
from functools import partial
import math

import jax
import jax.numpy as jnp
from jax import lax
from jax.experimental import pallas as pl
from jax.experimental.pallas import tpu as pltpu
from jax.sharding import PartitionSpec as P


QH = 32
KVH = 8
HD = 64
LEN = 1024
WIDTH = 2048
GROUP = QH // KVH
LANES = 128
TILE = 2 * LANES
ROW_STEP = 64
NEG = -1e30
DP, TENSOR = "dp", "tensor"
EPS = 1e-05
VMEM_LIMIT = 58 << 20


f32 = jnp.float32
bf16 = jnp.bfloat16


def dot(a, b, contract):
    return lax.dot_general(a, b, (contract, ((), ())), preferred_element_type=f32)


def ways_of(n):
    return 2 if WIDTH // n >= 2 * LANES else 1


def routes_of(n):
    bits = list(range(1, n.bit_length() - 1))
    return [bits, bits[::-1]][: ways_of(n)]


def block_slots(n):
    count, ways = n // 2, ways_of(n)
    return [(h, 0) for h in range(ways)] + [(h, s) for h in range(ways) for s in range(1, count)]


def width_order(n):
    routes, ways = routes_of(n), ways_of(n)
    order = []
    for core in range(2):
        for h, s in block_slots(n):
            j = core
            for t, b in enumerate(routes[h]):
                j |= ((s >> t) & 1) << b
            order.append(ways * j + h)
    return order


def swap(x, axis, n, b):
    return lax.ppermute(x, axis, [(i, i ^ (1 << b)) for i in range(n)])


def dp_gather(shard, n, cut=None):
    routes, ways = routes_of(n), ways_of(n)
    size = shard.shape[0] // ways
    parts = [[cut[h] if cut else shard[h * size : (h + 1) * size]] for h in range(ways)]
    for t in range(len(routes[0])):
        for h in range(ways):
            parts[h] += [swap(p, DP, n, routes[h][t]) for p in parts[h]]
    own = [shard] + [p for part in parts for p in part[1:]]
    return own + [swap(p, DP, n, 0) for p in own]


def scatter_segments(n):
    count, ways = n // 2, ways_of(n)
    size = WIDTH // n // ways
    half = count // 2
    cuts = [(ways + half - 1) * size, half * size]
    if ways > 1:
        cuts += [(half - 1) * size, half * size]
    return size, cuts


def add_kernel(*refs, spans):
    count = len(spans)
    for i, (at, rows, size) in enumerate(spans):
        kept, got, out = refs[2 * i], refs[2 * i + 1], refs[2 * count + i]
        total = kept[pl.ds(at, rows), :].astype(f32) + got[pl.ds(size, rows), :].astype(f32)
        out[...] = total.astype(bf16)


def add_rows(pairs, size):
    tile = 1024
    columns = pairs[0][0].shape[1]
    arrays = [x for array, _, _, got in pairs for x in (array, got)]
    return pl.pallas_call(
        partial(add_kernel, spans=[(at, rows, size) for _, at, rows, _ in pairs]),
        grid=(columns // tile,),
        in_specs=[pl.BlockSpec((x.shape[0], tile), lambda i: (0, i)) for x in arrays],
        out_specs=tuple(pl.BlockSpec((rows, tile), lambda i: (0, i)) for _, _, rows, _ in pairs),
        out_shape=tuple(jax.ShapeDtypeStruct((rows, columns), bf16) for _, _, rows, _ in pairs),
        compiler_params=pltpu.CompilerParams(vmem_limit_bytes=VMEM_LIMIT),
    )(*arrays)


def dp_scatter(pieces, n):
    routes, ways = routes_of(n), ways_of(n)
    size, _ = scatter_segments(n)
    kept = [(pieces[0], ways * size)] + ([(pieces[2], 0)] if ways > 1 else [])
    send = [pieces[1]] + ([pieces[3]] if ways > 1 else [])
    terms = [[] for _ in range(ways)]
    slots = n // 4
    for t in reversed(range(len(routes[0]))):
        for h in range(ways):
            terms[h].append(swap(send[h], DP, n, routes[h][t]))
        if t:
            rows = (slots - 1) * size
            sums = add_rows([(*kept[h], rows, terms[h][-1]) for h in range(ways)], size)
            slots //= 2
            send = [x[(slots - 1) * size :] if slots > 1 else x for x in sums]
            kept = [(x, 0) for x in sums]
    return pieces[0], terms


def width_at(order_ref, k, width):
    return pl.ds(pl.multiple_of(order_ref[k] * width, width), width)


def reorder_kernel(order_ref, *refs, inverse):
    ins, outs = refs[: len(refs) // 2], refs[len(refs) // 2 :]
    count = order_ref.shape[0]
    for src, dst in zip(ins, outs):
        width = src.shape[1] // count
        for k in range(count):
            here = pl.ds(k * width, width)
            if inverse:
                dst[:, width_at(order_ref, k, width)] = src[:, here]
            else:
                dst[:, here] = src[:, width_at(order_ref, k, width)]


SMEM_SPEC = pl.BlockSpec(memory_space=pltpu.SMEM)
VMEM_SPEC = pl.BlockSpec(memory_space=pltpu.VMEM)


def reorder(order, arrays, inverse):
    return pl.pallas_call(
        partial(reorder_kernel, inverse=inverse),
        out_shape=tuple(jax.ShapeDtypeStruct(a.shape, a.dtype) for a in arrays),
        in_specs=[SMEM_SPEC] + [VMEM_SPEC] * len(arrays),
        out_specs=tuple(VMEM_SPEC for _ in arrays),
    )(order, *arrays)


def rows_loop(count, body):
    step = min(ROW_STEP, count)

    def one(r, _):
        body(pl.ds(pl.multiple_of(r * step, step), step))
        return 0

    lax.fori_loop(0, count // step, one, 0)


def enter_kernel(order_ref, tok_ref, cot_ref, gain1_ref, gain2_ref, tok_out, cot_out, gain1_out, gain2_out, norm_ref):
    count = order_ref.shape[0]
    width = tok_ref.shape[1] // count
    for src, dst in ((tok_ref, tok_out), (cot_ref, cot_out), (gain1_ref, gain1_out), (gain2_ref, gain2_out)):
        for k in range(count):
            dst[:, k * width : (k + 1) * width] = src[:, width_at(order_ref, k, width)]

    def normalize(at):
        values = tok_out[at, :].astype(f32)
        inverse = lax.rsqrt(jnp.mean(values * values, axis=1, keepdims=True) + EPS)
        norm_ref[at, :] = (values * inverse * gain1_out[...]).astype(bf16)

    rows_loop(tok_ref.shape[0], normalize)


def enter(order, tokens, cotangent, gain1, gain2):
    arrays = (tokens, cotangent, gain1, gain2)
    return pl.pallas_call(
        enter_kernel,
        out_shape=tuple(jax.ShapeDtypeStruct(a.shape, a.dtype) for a in (*arrays, tokens)),
        in_specs=[SMEM_SPEC] + [VMEM_SPEC] * 4,
        out_specs=tuple(VMEM_SPEC for _ in range(5)),
        name="ro",
    )(order, *arrays)


def unpack_kernel(me_ref, *refs, groups, counts):
    ins, outs = refs[:counts], refs[counts:]
    per = len(outs) // groups
    rows = outs[0].shape[0]
    cuts = [x[pl.ds(k * rows, rows), :] for x in ins for k in range(x.shape[0] // rows)]
    for s, cut in enumerate(cuts):
        for i in range(groups):
            mine = outs[i * per : (i + 1) * per]
            width = cut.shape[1] // groups
            value = cut[:, i * width : (i + 1) * width]
            if counts > 1:
                z = jnp.bitwise_xor(me_ref[0], s)
                at = pl.ds(pl.multiple_of(z * width, width), width)
            else:
                at = pl.ds(s * width, width)
            mine[0][:, at] = value
            size = rows // max(1, per - 1)
            for h in range(per - 1):
                mine[h + 1][:, at] = value[h * size : (h + 1) * size]


def unpack(me, cuts, groups, n_tensor, ways):
    rows = sum(x.shape[0] for x in cuts) // n_tensor
    columns = cuts[0].shape[1] // groups * n_tensor
    shapes = [(rows, columns)] + [(rows // ways, columns)] * ways
    outs = pl.pallas_call(
        partial(unpack_kernel, groups=groups, counts=len(cuts)),
        out_shape=tuple(jax.ShapeDtypeStruct(x, bf16) for x in shapes * groups),
        in_specs=[SMEM_SPEC] + [VMEM_SPEC] * len(cuts),
        out_specs=tuple(VMEM_SPEC for _ in shapes * groups),
    )(me, *cuts)
    per = len(shapes)
    return [(outs[i * per], outs[i * per + 1 : (i + 1) * per]) for i in range(groups)]


def shard_sum(first_ref, terms, ways, at):
    parts = []
    for h in range(ways):
        size = terms[h][-1].shape[0]
        total = first_ref[pl.ds(h * size, size), at].astype(f32)
        for t in terms[h]:
            total = total + t[pl.ds(0, size), at].astype(f32)
        parts.append(total)
    return parts[0] if ways == 1 else jnp.concatenate(parts, axis=0)


def transpose_kernel(in_ref, out_ref, *parts):
    value = in_ref[...].T
    out_ref[...] = value
    for h, part in enumerate(parts):
        part[...] = value[h * part.shape[0] : (h + 1) * part.shape[0]]


def beside_kernel(left_ref, right_ref, out_ref):
    columns = left_ref.shape[1]
    out_ref[:, :columns] = left_ref[...]
    out_ref[:, columns:] = right_ref[...].T


def beside(left, right):
    return pl.pallas_call(
        beside_kernel,
        out_shape=jax.ShapeDtypeStruct((left.shape[0], left.shape[1] + right.shape[0]), left.dtype),
        in_specs=[VMEM_SPEC, VMEM_SPEC],
        out_specs=VMEM_SPEC,
        name="cq",
    )(left, right)


def transposed(x, ways):
    columns, rows = x.shape
    shapes = [(rows, columns)] + [(rows // ways, columns)] * ways
    out, *parts = pl.pallas_call(
        transpose_kernel,
        out_shape=tuple(jax.ShapeDtypeStruct(y, x.dtype) for y in shapes),
        in_specs=[VMEM_SPEC],
        out_specs=tuple(VMEM_SPEC for _ in shapes),
    )(x)
    return out, parts


def split_terms(refs, ways):
    each = len(refs) // ways
    return [refs[h * each : (h + 1) * each] for h in range(ways)]


def flat(scattered):
    first, terms = scattered
    return [first] + [t for part in terms for t in part]


def pack_kernel(*refs, n_tensor, ways, groups):
    out_ref = refs[-1]
    rows = out_ref.shape[0] // n_tensor
    count = (len(refs) - 1) // len(groups)
    for i, cuts in enumerate(groups):
        mine = refs[i * count : (i + 1) * count]
        terms = split_terms(mine[1:], ways)
        for at, width, starts in cuts:
            for z in range(n_tensor):
                total = shard_sum(mine[0], terms, ways, pl.ds(starts[z], width))
                out_ref[pl.ds(z * rows, rows), pl.ds(at, width)] = total.astype(out_ref.dtype)


def pack(scattered, groups, n_tensor, ways, columns, rows):
    arrays = [a for s in scattered for a in flat(s)]
    return pl.pallas_call(
        partial(pack_kernel, n_tensor=n_tensor, ways=ways, groups=groups),
        out_shape=jax.ShapeDtypeStruct((n_tensor * rows, columns), bf16),
        in_specs=[VMEM_SPEC] * len(arrays),
        out_specs=VMEM_SPEC,
        compiler_params=pltpu.CompilerParams(vmem_limit_bytes=VMEM_LIMIT),
    )(*arrays)


def final_kernel(*refs, ways, outs, transposed):
    outputs = refs[-outs:]
    refs = refs[:-outs]
    total = shard_sum(refs[0], split_terms(refs[1:], ways), ways, slice(None))
    total = total.T if transposed else total
    each = pl.num_programs(0) // outs
    for k, out in enumerate(outputs):

        @pl.when(pl.program_id(0) // each == k)
        def _(out=out):
            out[...] = total


def finish(scattered, columns, outs, ways, transposed):
    arrays = flat(scattered)
    size = scattered[1][0][-1].shape[0]
    rows = ways * size
    tile = 512
    each = columns // tile
    blocks = [rows] + [size] * (len(arrays) - 1)
    at = [partial(lambda i, k: jnp.clip(i - k * each, 0, each - 1), k=k) for k in range(outs)]
    specs = [
        pl.BlockSpec((tile, rows), partial(lambda i, f: (f(i), 0), f=f))
        if transposed
        else pl.BlockSpec((rows, tile), partial(lambda i, f: (0, f(i)), f=f))
        for f in at
    ]
    return pl.pallas_call(
        partial(final_kernel, ways=ways, outs=outs, transposed=transposed),
        grid=(outs * each,),
        out_shape=tuple(jax.ShapeDtypeStruct((columns, rows) if transposed else (rows, columns), f32) for _ in at),
        in_specs=[pl.BlockSpec((b, tile), lambda i: (0, i)) for b in blocks],
        out_specs=tuple(specs),
    )(*arrays)


def joined(refs):
    return jnp.concatenate([r[...] for r in refs], axis=0)


def piece_specs(pieces, tile, column):
    return [pl.BlockSpec((p.shape[0], tile), lambda i, *_: (0, column(i))) for p in pieces]


def tables_kernel(row0_ref, cos_ref, sin_ref, all_cos_ref, all_sin_ref, own_cos_ref, own_sin_ref):
    repeat = LANES // cos_ref.shape[1]
    cosine, sine = cos_ref[...], sin_ref[...]
    all_cos_ref[...] = jnp.concatenate([cosine] * repeat, axis=1)
    all_sin_ref[...] = jnp.concatenate([-sine, sine] * (repeat // 2), axis=1)
    own = pl.ds(pl.multiple_of(row0_ref[0], own_cos_ref.shape[0]), own_cos_ref.shape[0])
    own_cos_ref[...] = all_cos_ref[own, :]
    own_sin_ref[...] = all_sin_ref[own, :]


def rotary_tables(row0, cosine, sine, rows):
    shapes = [(cosine.shape[0], LANES)] * 2 + [(rows, LANES)] * 2
    return pl.pallas_call(
        tables_kernel,
        out_shape=tuple(jax.ShapeDtypeStruct(x, f32) for x in shapes),
        in_specs=[SMEM_SPEC, VMEM_SPEC, VMEM_SPEC],
        out_specs=tuple(VMEM_SPEC for _ in shapes),
        name="tb",
    )(row0, cosine, sine)


def swap_halves(u):
    lane = lax.broadcasted_iota(jnp.int32, u.shape, 1)
    up = pltpu.roll(u, HD // 2, 1)
    down = pltpu.roll(u, LANES - HD // 2, 1)
    return jnp.where((lane % HD) < HD // 2, down, up)


def turn(u, cosine, signed_sine, back):
    s = swap_halves(u) * signed_sine
    return u * cosine - s if back else u * cosine + s


def proj_kv_kernel(x_ref, cos_ref, sin_ref, *refs):
    out_ref = refs[-1]
    raw = dot(x_ref[...], joined(refs[:-1]), ((1,), (0,)))
    out_ref[:, :LANES] = turn(raw[:, :LANES], cos_ref[...], sin_ref[...], False).astype(bf16)
    out_ref[:, LANES:] = raw[:, LANES:].astype(bf16)


def proj_kv(x, cosine, sine, pieces):
    rows = x.shape[0]
    whole = lambda shape: pl.BlockSpec(shape, lambda i: (0, 0))
    return pl.pallas_call(
        proj_kv_kernel,
        grid=(2 * KVH * HD // TILE,),
        in_specs=[whole(x.shape), whole(cosine.shape), whole(sine.shape)] + piece_specs(pieces, TILE, lambda i: i),
        out_specs=pl.BlockSpec((rows, TILE), lambda i: (0, i)),
        out_shape=jax.ShapeDtypeStruct((rows, 2 * KVH * HD), bf16),
        cost_estimate=pl.CostEstimate(flops=4 * rows * WIDTH * KVH * HD, bytes_accessed=6 << 20, transcendentals=0),
        compiler_params=pltpu.CompilerParams(vmem_limit_bytes=VMEM_LIMIT),
        name="pk",
    )(x, cosine, sine, *pieces)


def split_halves(block, odd):
    wide = block.astype(f32)
    rolled = pltpu.roll(wide, HD, 1)
    lane = lax.broadcasted_iota(jnp.int32, wide.shape, 1)
    low = lane < HD
    first = jnp.where(odd, rolled, wide)
    second = jnp.where(odd, wide, rolled)
    zero = jnp.zeros_like(wide)
    return jnp.where(low, first, zero).astype(bf16), jnp.where(low, zero, second).astype(bf16)


def attn_fwd_kernel(row0_ref, seg_ref, x_ref, k_ref, v_ref, cos_ref, sin_ref, *refs, count):
    w_query = refs[:count]
    ctx_ref, rot_ref, lse_ref, bias_ref = refs[-4:]
    g = pl.program_id(0)
    rows = x_ref.shape[0]

    @pl.when(g == 0)
    def _():
        t = row0_ref[0] + lax.broadcasted_iota(jnp.int32, bias_ref.shape, 0)
        s = lax.broadcasted_iota(jnp.int32, bias_ref.shape, 1)
        allowed = (s <= t) & (s >= seg_ref[...])
        bias_ref[...] = jnp.where(allowed, 0.0, NEG)

    q_raw = dot(x_ref[...], joined(w_query), ((1,), (0,)))
    odd = lax.rem(g, 2) == 1
    keys = split_halves(k_ref[...], odd)
    values = split_halves(v_ref[...], odd)
    lane = lax.broadcasted_iota(jnp.int32, (rows, LANES), 1)
    log_sums = jnp.zeros((rows, LANES), f32)
    for c in range(GROUP // 2):
        at = pl.ds(c * LANES, LANES)
        turned = turn(q_raw[:, c * LANES : (c + 1) * LANES], cos_ref[...], sin_ref[...], False)
        query = (turned * (HD**-0.5)).astype(bf16)
        rot_ref[:, at] = query
        total = jnp.zeros((rows, LANES), f32)
        for e in range(2):
            scores = dot(query, keys[e], ((1,), (1,))) + bias_ref[...]
            peak = jnp.max(scores, axis=1, keepdims=True)
            weights = jnp.exp(scores - peak)
            mass = jnp.sum(weights, axis=1, keepdims=True)
            part = dot(weights.astype(bf16), values[e], ((1,), (0,)))
            total = total + part * (1.0 / mass)
            log_sums = jnp.where(lane == 2 * c + e, peak + jnp.log(mass), log_sums)
        ctx_ref[:, at] = total.astype(bf16)
    lse_ref[...] = log_sums


FWD_PARTS = 2


def attn_forward(row0, seg_col, x, kv, cosine, sine, pieces, part, before):
    rows = x.shape[0]
    heads = KVH // FWD_PARTS
    base = part * heads
    args = [row0, seg_col, x, kv, kv, cosine, sine, *pieces]
    whole = lambda shape: pl.BlockSpec(shape, lambda g, r: (0, 0))
    grid_spec = pltpu.PrefetchScalarGridSpec(
        num_scalar_prefetch=1,
        grid=(heads,),
        in_specs=[
            whole((rows, 1)),
            whole(x.shape),
            pl.BlockSpec((LEN, LANES), lambda g, r: (0, (base + g) // 2 * 2)),
            pl.BlockSpec((LEN, LANES), lambda g, r: (0, (base + g) // 2 * 2 + 1)),
            whole((rows, LANES)),
            whole((rows, LANES)),
        ]
        + piece_specs(pieces, TILE, lambda g: base + g)
        + [pl.BlockSpec(memory_space=pl.ANY)] * len(before),
        out_specs=[
            pl.BlockSpec((rows, TILE), lambda g, r: (0, base + g)),
            pl.BlockSpec((rows, TILE), lambda g, r: (0, base + g)),
            pl.BlockSpec((rows, LANES), lambda g, r: (0, base + g)),
        ],
        scratch_shapes=[pltpu.VMEM((rows, LEN), f32)],
    )
    return pl.pallas_call(
        partial(attn_fwd_kernel, count=len(pieces)),
        grid_spec=grid_spec,
        out_shape=(
            jax.ShapeDtypeStruct((rows, QH * HD), bf16),
            jax.ShapeDtypeStruct((rows, QH * HD), bf16),
            jax.ShapeDtypeStruct((rows, KVH * LANES), f32),
        ),
        cost_estimate=pl.CostEstimate(
            flops=8 * rows * LEN * QH * HD, bytes_accessed=12 << 20, transcendentals=rows * LEN * QH // FWD_PARTS
        ),
        compiler_params=pltpu.CompilerParams(vmem_limit_bytes=VMEM_LIMIT),
        input_output_aliases={len(args) + i: i for i in range(len(before))},
    )(*args, *before)


def out_proj_kernel(ctx_ref, tok_ref, gain_ref, *refs):
    mid_ref, first_ref, second_ref, sum_ref = refs[-4:]
    i = pl.program_id(0)

    @pl.when(i == 0)
    def _():
        sum_ref[...] = tok_ref[...].astype(f32)

    sum_ref[...] += dot(ctx_ref[...], joined(refs[:-4]), ((1,), (1,)))

    @pl.when(i == pl.num_programs(0) - 1)
    def _():
        half = first_ref.shape[0]
        step = min(ROW_STEP, half)

        for k, out_ref in enumerate((first_ref, second_ref)):

            def body(r, _, k=k, out_ref=out_ref):
                at = pl.ds(pl.multiple_of(k * half + r * step, step), step)
                middle = sum_ref[at, :]
                mid_ref[at, :] = middle
                inverse = lax.rsqrt(jnp.mean(middle * middle, axis=1, keepdims=True) + EPS)
                out_ref[pl.ds(pl.multiple_of(r * step, step), step), :] = (middle * inverse * gain_ref[...]).astype(bf16)
                return 0

            lax.fori_loop(0, half // step, body, 0)


def out_proj(context, tokens, gain, pieces):
    rows = context.shape[0]
    tile = 512
    whole = lambda shape: pl.BlockSpec(shape, lambda i: (0, 0))
    return pl.pallas_call(
        out_proj_kernel,
        grid=(QH * HD // tile,),
        in_specs=[pl.BlockSpec((rows, tile), lambda i: (0, i)), whole(tokens.shape), whole(gain.shape)]
        + piece_specs(pieces, tile, lambda i: i),
        out_specs=(whole((rows, WIDTH)), whole((rows // 2, WIDTH)), whole((rows // 2, WIDTH))),
        out_shape=(
            jax.ShapeDtypeStruct((rows, WIDTH), f32),
            jax.ShapeDtypeStruct((rows // 2, WIDTH), bf16),
            jax.ShapeDtypeStruct((rows // 2, WIDTH), bf16),
        ),
        scratch_shapes=[pltpu.VMEM((rows, WIDTH), f32)],
        cost_estimate=pl.CostEstimate(flops=2 * rows * WIDTH * QH * HD, bytes_accessed=14 << 20, transcendentals=0),
        compiler_params=pltpu.CompilerParams(vmem_limit_bytes=VMEM_LIMIT),
        name="op",
    )(context, tokens, gain, *pieces)


def rms_back(values, gain, grad):
    inverse = lax.rsqrt(jnp.mean(values * values, axis=1, keepdims=True) + EPS)
    scaled = gain * grad
    along = jnp.mean(scaled * values, axis=1, keepdims=True)
    d_values = inverse * scaled - values * (inverse * inverse * inverse) * along
    d_gain = jnp.sum(grad * values * inverse, axis=0, keepdims=True)
    return d_values, d_gain


def mid_back_kernel(mid_ref, gain_ref, cot_ref, *refs):
    dmid_ref, db_ref, dg_ref = refs[-3:]
    each = refs[0].shape[0]
    step = min(ROW_STEP, each)
    dg_ref[...] = jnp.zeros_like(dg_ref)

    for k, dn_ref in enumerate(refs[:-3]):

        def body(r, _, k=k, dn_ref=dn_ref):
            at = pl.ds(pl.multiple_of(k * each + r * step, step), step)
            grad = dn_ref[pl.ds(pl.multiple_of(r * step, step), step), :].astype(f32)
            d_values, d_gain = rms_back(mid_ref[at, :], gain_ref[...], grad)
            d_middle = cot_ref[at, :].astype(f32) + d_values
            dmid_ref[at, :] = d_middle
            db_ref[at, :] = d_middle.astype(bf16)
            dg_ref[0:1, :] += d_gain
            return 0

        lax.fori_loop(0, each // step, body, 0)


def mid_back(d_normed, middle, gain, cot):
    rows = middle.shape[0]
    return pl.pallas_call(
        mid_back_kernel,
        out_shape=(
            jax.ShapeDtypeStruct((rows, WIDTH), f32),
            jax.ShapeDtypeStruct((rows, WIDTH), bf16),
            jax.ShapeDtypeStruct((8, WIDTH), f32),
        ),
        name="mb",
    )(middle, gain, cot, *d_normed)


def attn_bwd_kernel(
    row0_ref, seg_ref, q_ref, k_ref, v_ref, db_ref, ctx_ref, lse_ref, cos_ref, sin_ref, all_cos_ref, all_sin_ref, *refs, count
):
    w_query, w_out = refs[:count], refs[count : 2 * count]
    dq_ref, dkv_ref, dn_ref, bias_ref = refs[2 * count :]
    g = pl.program_id(0)
    rows = q_ref.shape[0]

    @pl.when(g == 0)
    def _():
        s = lax.broadcasted_iota(jnp.int32, bias_ref.shape, 0)
        t = row0_ref[0] + lax.broadcasted_iota(jnp.int32, bias_ref.shape, 1)
        allowed = (s <= t) & (s >= seg_ref[...])
        bias_ref[...] = jnp.where(allowed, 0.0, NEG)
        dn_ref[...] = jnp.zeros_like(dn_ref)

    d_context = dot(db_ref[...], joined(w_out), ((1,), (0,))).astype(bf16)
    odd = lax.rem(g, 2) == 1
    keys = split_halves(k_ref[...], odd)
    values = split_halves(v_ref[...], odd)
    log_sums = lse_ref[...].T
    low = lax.broadcasted_iota(jnp.int32, (rows, LANES), 1) < HD
    dk_sum = jnp.zeros((LEN, LANES), f32)
    dv_sum = jnp.zeros((LEN, LANES), f32)
    for c in range(GROUP // 2):
        at = pl.ds(c * LANES, LANES)
        query, d_rows = q_ref[:, at], d_context[:, c * LANES : (c + 1) * LANES]
        both = (d_rows.astype(f32) * ctx_ref[:, at].astype(f32)).T
        dq = jnp.zeros((rows, LANES), f32)
        for e in range(2):
            mine = low if e == 0 else jnp.logical_not(low)
            delta = jnp.sum(both[e * HD : (e + 1) * HD], axis=0, keepdims=True)
            h = 2 * c + e
            scores = dot(keys[e], query, ((1,), (1,))) + bias_ref[...]
            probs = jnp.exp(scores - log_sums[h : h + 1])
            d_probs = dot(values[e], d_rows, ((1,), (1,)))
            d_scores = (probs * (d_probs - delta)).astype(bf16)
            zero = jnp.zeros_like(query)
            dv_sum = dv_sum + dot(probs.astype(bf16), jnp.where(mine, d_rows, zero), ((1,), (0,)))
            dk_sum = dk_sum + dot(d_scores, jnp.where(mine, query, zero), ((1,), (0,)))
            dq = dq + dot(d_scores, keys[e], ((0,), (0,)))
        dq_ref[:, at] = turn(dq * (HD**-0.5), cos_ref[...], sin_ref[...], True).astype(bf16)
    dn_ref[...] += dot(dq_ref[...], joined(w_query), ((1,), (1,)))
    wide_low = lax.broadcasted_iota(jnp.int32, (LEN, LANES), 1) < HD
    keep = wide_low == odd
    dk_sum = turn(dk_sum + pltpu.roll(dk_sum, HD, 1), all_cos_ref[...], all_sin_ref[...], True)
    dv_sum = dv_sum + pltpu.roll(dv_sum, HD, 1)
    for i, total in enumerate((dk_sum, dv_sum)):
        at = pl.ds(i * LANES, LANES)
        dkv_ref[:, at] = jnp.where(keep, dkv_ref[:, at], total.astype(bf16))


def attn_backward(row0, seg_row, query, kv, d_branch, context, lse, cosine, sine, all_cosine, all_sine, q_pieces, out_pieces):
    rows = query.shape[0]
    whole = lambda shape: pl.BlockSpec(shape, lambda g, r: (0, 0))
    grid_spec = pltpu.PrefetchScalarGridSpec(
        num_scalar_prefetch=1,
        grid=(KVH,),
        in_specs=[
            whole((1, rows)),
            pl.BlockSpec((rows, TILE), lambda g, r: (0, g)),
            pl.BlockSpec((LEN, LANES), lambda g, r: (0, g // 2 * 2)),
            pl.BlockSpec((LEN, LANES), lambda g, r: (0, g // 2 * 2 + 1)),
            whole((rows, WIDTH)),
            pl.BlockSpec((rows, TILE), lambda g, r: (0, g)),
            pl.BlockSpec((rows, LANES), lambda g, r: (0, g)),
            whole((rows, LANES)),
            whole((rows, LANES)),
            whole((LEN, LANES)),
            whole((LEN, LANES)),
        ]
        + piece_specs(q_pieces, TILE, lambda g: g)
        + piece_specs(out_pieces, TILE, lambda g: g),
        out_specs=[
            pl.BlockSpec((rows, TILE), lambda g, r: (0, g)),
            pl.BlockSpec((LEN, TILE), lambda g, r: (0, g // 2)),
            whole((rows, WIDTH)),
        ],
        scratch_shapes=[pltpu.VMEM((LEN, rows), f32)],
    )
    return pl.pallas_call(
        partial(attn_bwd_kernel, count=len(q_pieces)),
        grid_spec=grid_spec,
        out_shape=(
            jax.ShapeDtypeStruct((rows, QH * HD), bf16),
            jax.ShapeDtypeStruct((LEN, 2 * KVH * HD), bf16),
            jax.ShapeDtypeStruct((rows, WIDTH), f32),
        ),
        cost_estimate=pl.CostEstimate(
            flops=28 * rows * LEN * QH * HD, bytes_accessed=28 << 20, transcendentals=rows * LEN * QH
        ),
        compiler_params=pltpu.CompilerParams(vmem_limit_bytes=VMEM_LIMIT),
        name="ab",
    )(row0, seg_row, query, kv, kv, d_branch, context, lse, cosine, sine, all_cosine, all_sine, *q_pieces, *out_pieces)


def in_back_kernel(order_ref, dkv_ref, part_ref, tok_ref, gain_ref, dmid_ref, dg_mlp_ref, *refs):
    out_ref, dg_ref, sum_ref, gain_ref_sum = refs[-4:]
    i = pl.program_id(0)

    @pl.when(i == 0)
    def _():
        sum_ref[...] = part_ref[...]
        dg_ref[...] = jnp.zeros_like(dg_ref)

    sum_ref[...] += dot(dkv_ref[...], joined(refs[:-4]), ((1,), (1,)))

    @pl.when(i == pl.num_programs(0) - 1)
    def _():
        count = order_ref.shape[0]
        width = sum_ref.shape[1] // count
        gain_ref_sum[...] = jnp.zeros_like(gain_ref_sum)

        def body(at):
            d_values, d_gain = rms_back(tok_ref[at, :].astype(f32), gain_ref[...], sum_ref[at, :])
            d_values = d_values + dmid_ref[at, :]
            gain_ref_sum[0:1, :] += d_gain
            for k in range(count):
                out_ref[at, width_at(order_ref, k, width)] = d_values[:, k * width : (k + 1) * width]

        rows_loop(sum_ref.shape[0], body)
        for k in range(count):
            at = width_at(order_ref, k, width)
            here = pl.ds(k * width, width)
            dg_ref[0:1, at] = gain_ref_sum[0:1, here]
            dg_ref[1:2, at] = dg_mlp_ref[0:1, here]


def in_back(order, d_kv, part, tokens, gain, d_middle, mlp_gain, pieces):
    rows = tokens.shape[0]
    whole = lambda shape: pl.BlockSpec(shape, lambda i: (0, 0))
    return pl.pallas_call(
        in_back_kernel,
        grid=(2 * KVH * HD // TILE,),
        in_specs=[SMEM_SPEC, pl.BlockSpec((rows, TILE), lambda i: (0, i))]
        + [whole(a.shape) for a in (part, tokens, gain, d_middle, mlp_gain)]
        + piece_specs(pieces, TILE, lambda i: i),
        out_specs=(whole((rows, WIDTH)), whole((8, WIDTH))),
        out_shape=(jax.ShapeDtypeStruct((rows, WIDTH), f32), jax.ShapeDtypeStruct((8, WIDTH), f32)),
        scratch_shapes=[pltpu.VMEM((rows, WIDTH), f32), pltpu.VMEM((8, WIDTH), f32)],
        cost_estimate=pl.CostEstimate(flops=4 * rows * WIDTH * KVH * HD, bytes_accessed=16 << 20, transcendentals=0),
        compiler_params=pltpu.CompilerParams(vmem_limit_bytes=VMEM_LIMIT),
        name="ib",
    )(order, d_kv, part, tokens, gain, d_middle, mlp_gain, *pieces)


def d_hidden_kernel(me_ref, *refs, slots):
    cots, pieces = refs[: 2 * slots - 1], refs[2 * slots - 1 : -3]
    out_ref, first_ref, second_ref = refs[-3:]
    half = cots[0].shape[0] // 2

    @pl.when(pl.program_id(0) == 0)
    def _():
        for r in range(slots):
            z = lax.rem(me_ref[0] - r + slots, slots)
            at = pl.ds(pl.multiple_of(z * half, half), half)
            for k, whole_ref in enumerate((first_ref, second_ref)):
                here = pl.ds(k * half, half)
                value = cots[r][here, :] + cots[2 * slots - 1 - r][here, :] if r else cots[0][here, :]
                whole_ref[at, :] = value

    weights = joined(pieces)
    rows = first_ref.shape[0]
    out_ref[:rows, :] = dot(first_ref[...], weights, ((1,), (0,)))
    out_ref[rows:, :] = dot(second_ref[...], weights, ((1,), (0,)))


def d_hidden_of(me, cots, pieces):
    slots = (len(cots) + 1) // 2
    rows = cots[0].shape[0] * slots
    ff = pieces[0].shape[1]
    whole = lambda shape: pl.BlockSpec(shape, lambda i: (0, 0))
    half = (rows // 2, WIDTH)
    return pl.pallas_call(
        partial(d_hidden_kernel, slots=slots),
        grid=(ff // TILE,),
        in_specs=[SMEM_SPEC] + [whole(c.shape) for c in cots] + piece_specs(pieces, TILE, lambda i: i),
        out_specs=(pl.BlockSpec((rows, TILE), lambda i: (0, i)), whole(half), whole(half)),
        out_shape=(
            jax.ShapeDtypeStruct((rows, ff), f32),
            jax.ShapeDtypeStruct(half, bf16),
            jax.ShapeDtypeStruct(half, bf16),
        ),
        cost_estimate=pl.CostEstimate(flops=2 * rows * WIDTH * ff, bytes_accessed=24 << 20, transcendentals=0),
        compiler_params=pltpu.CompilerParams(vmem_limit_bytes=VMEM_LIMIT),
        name="dh",
    )(me, *cots, *pieces)


def mlp_kernel(x_ref, dh_ref, *refs, count):
    hidden_ref, grads_ref = refs[2 * count :]
    gate = dot(x_ref[...], joined(refs[:count]), ((1,), (0,)))
    up = dot(x_ref[...], joined(refs[count : 2 * count]), ((1,), (0,)))
    d_hidden = dh_ref[...]
    sig = jax.nn.sigmoid(gate)
    silu = gate * sig
    hidden_ref[...] = (silu * up).astype(bf16)
    grads_ref[0] = (d_hidden * up * (sig + silu * (1.0 - sig))).astype(bf16)
    grads_ref[1] = (d_hidden * silu).astype(bf16)


def mlp(x, d_hidden, chunk, pieces):
    rows = x.shape[0]
    ff = d_hidden.shape[1]
    tiles = ff // TILE
    specs = [pl.BlockSpec((rows, WIDTH), lambda i: (0, 0)), pl.BlockSpec((rows, TILE), lambda i: (chunk, i))]
    for base in (0, tiles):
        specs += piece_specs(pieces, TILE, partial(lambda i, base: base + i, base=base))
    return pl.pallas_call(
        partial(mlp_kernel, count=len(pieces)),
        grid=(tiles,),
        in_specs=specs,
        out_specs=(pl.BlockSpec((rows, TILE), lambda i: (0, i)), pl.BlockSpec((2, rows, TILE), lambda i: (0, 0, i))),
        out_shape=(jax.ShapeDtypeStruct((rows, ff), bf16), jax.ShapeDtypeStruct((2, rows, ff), bf16)),
        cost_estimate=pl.CostEstimate(flops=4 * rows * WIDTH * ff, bytes_accessed=30 << 20, transcendentals=rows * ff),
        compiler_params=pltpu.CompilerParams(vmem_limit_bytes=VMEM_LIMIT),
    )(x, d_hidden, *pieces, *pieces)


def back_kernel(x_ref, *refs):
    out_ref, sum_ref = refs[-2:]
    i = pl.program_id(0)
    rows = sum_ref.shape[0]

    @pl.when(i == 0)
    def _():
        def clear(at):
            sum_ref[at, :] = jnp.zeros((at.size, sum_ref.shape[1]), f32)

        rows_loop(rows, clear)

    sum_ref[...] += dot(x_ref[...].reshape(x_ref.shape[-2:]), joined(refs[:-2]), ((1,), (1,)))

    @pl.when(i == pl.num_programs(0) - 1)
    def _():
        def write(at):
            out_ref[at, :] = sum_ref[at, :].astype(bf16)

        rows_loop(rows, write)


def back(x, pieces):
    many, rows, ff = x.shape
    tile = min(1024, ff)
    per = ff // tile
    return pl.pallas_call(
        back_kernel,
        grid=(many * per,),
        in_specs=[pl.BlockSpec((1, rows, tile), lambda i: (i // per, 0, i % per))]
        + piece_specs(pieces, tile, lambda i: i),
        out_specs=pl.BlockSpec((rows, WIDTH), lambda i: (0, 0)),
        out_shape=jax.ShapeDtypeStruct((rows, WIDTH), bf16),
        scratch_shapes=[pltpu.VMEM((rows, WIDTH), f32)],
        cost_estimate=pl.CostEstimate(flops=2 * many * rows * WIDTH * ff, bytes_accessed=(12 << 20) * many, transcendentals=0),
        compiler_params=pltpu.CompilerParams(vmem_limit_bytes=VMEM_LIMIT),
    )(x, *pieces)


def grad_kernel(*refs, chunks, received, cuts):
    lefts, rights = refs[:chunks], refs[chunks : 2 * chunks]
    outs, turned_ref = refs[2 * chunks + received : -1], refs[-1]

    @pl.when(pl.program_id(0) == 0)
    def _():
        depth = lefts[0].shape[0]
        for c, left in enumerate(lefts):
            turned_ref[:, pl.ds(c * depth, depth)] = left[...].T

    right = jnp.concatenate([r[...].reshape(r.shape[-2:]) for r in rights], axis=0)
    total = dot(turned_ref[...], right, ((1,), (0,)))
    if received:
        total = total + refs[2 * chunks][...].astype(f32)
    at = 0
    for out, rows in zip(outs, cuts):
        out[...] = total[at : at + rows].astype(bf16)
        at += rows


def weight_grad(lefts, rights, which, block, got, cuts):
    _, depth, columns = rights[0].shape
    rows = WIDTH // 2
    tile = min(512, columns)
    chunks = len(lefts)
    column = lambda i: (0, i)
    extra = [got] if got is not None else []
    specs = [pl.BlockSpec((depth, rows), lambda i: (0, block))] * chunks
    specs += [pl.BlockSpec((1, depth, tile), lambda i: (which, 0, i))] * chunks
    specs += [pl.BlockSpec((rows, tile), column)] * len(extra)
    return pl.pallas_call(
        partial(grad_kernel, chunks=chunks, received=len(extra), cuts=cuts),
        grid=(columns // tile,),
        in_specs=specs,
        out_specs=tuple(pl.BlockSpec((c, tile), column) for c in cuts),
        out_shape=tuple(jax.ShapeDtypeStruct((c, columns), bf16) for c in cuts),
        scratch_shapes=[pltpu.VMEM((rows, depth * chunks), bf16)],
        cost_estimate=pl.CostEstimate(
            flops=2 * rows * depth * chunks * columns, bytes_accessed=8 * rows * columns, transcendentals=0
        ),
        compiler_params=pltpu.CompilerParams(vmem_limit_bytes=VMEM_LIMIT),
    )(*lefts, *rights, *extra)


def over_tensor(x, axis=0):
    return lax.all_gather(x, TENSOR, axis=axis, tiled=True)


def sum_tensor(x):
    return lax.psum_scatter(x, TENSOR, scatter_dimension=0, tiled=True)


def layer(
    tokens, segments, positions, norm_attn, w_query, w_key, w_value, w_out,
    norm_mlp, w_gate, w_up, w_down, cotangent, *, n_dp, n_tensor,
):
    me_dp, me_z = lax.axis_index(DP), lax.axis_index(TENSOR)
    rows, width = tokens.shape
    assert rows * n_tensor == LEN and width == WIDTH
    kv, q = w_key.shape[1], w_query.shape[1]
    ways = ways_of(n_dp)
    ff = w_gate.shape[1]
    order = jnp.bitwise_xor(jnp.array(width_order(n_dp), jnp.int32), ways * me_dp)
    row0 = (me_z * rows).reshape(1)
    own_segs = lax.dynamic_slice_in_dim(segments, me_z * rows, rows, 0)

    if kv % LANES == 0:
        slots = [jnp.concatenate([w_key, w_value], axis=1)]
        for b in range(n_tensor.bit_length() - 1):
            slots.append(swap(jnp.concatenate(slots, axis=0), TENSOR, n_tensor, b))
        kv_rows, kv_cut = unpack(me_z.reshape(1), slots, 1, n_tensor, ways)[0]
    else:
        pairs = [over_tensor(w, 1).reshape(w.shape[0], -1, LANES) for w in (w_key, w_value)]
        kv_rows, kv_cut = jnp.concatenate(pairs, axis=2).reshape(w_key.shape[0], -1), None
    kv_pieces = dp_gather(kv_rows, n_dp, kv_cut)
    both = over_tensor(beside(w_query, w_out))
    (q_rows, q_cut), (out_rows, out_cut) = unpack(me_z.reshape(1), [both], 2, n_tensor, ways)
    q_pieces = dp_gather(q_rows, n_dp, q_cut)
    out_pieces = dp_gather(out_rows, n_dp, out_cut)
    gu_pieces = dp_gather(jnp.concatenate([w_gate, w_up], axis=1), n_dp)
    down_rows, down_cut = transposed(w_down, ways)
    down_pieces = dp_gather(down_rows, n_dp, down_cut)

    tokens_here, cot_here, gain_attn, gain_mlp, normed_local = enter(
        order, tokens, cotangent, norm_attn[None], norm_mlp[None]
    )
    below, above = [cot_here], [cot_here]
    for r in range(1, n_tensor):
        below.append(lax.ppermute(below[-1], TENSOR, [(i, i + 1) for i in range(r - 1, n_tensor - 1)]))
        above.append(lax.ppermute(above[-1], TENSOR, [(i + 1, i) for i in range(n_tensor - r)]))
    cots = below + above[1:]

    freq_index = jnp.arange(HD // 2, dtype=jnp.int32).astype(f32)
    inverse = jnp.exp(freq_index * (-2.0 * math.log(500000.0) / HD))
    angles = positions.astype(f32)[:, None] * inverse[None, :]
    all_cosine, all_sine, cosine, sine = rotary_tables(row0, jnp.cos(angles), jnp.sin(angles), rows)

    kv_all = over_tensor(proj_kv(normed_local, cosine, sine, kv_pieces))
    attended = ()
    for i in range(FWD_PARTS):
        attended = attn_forward(row0, own_segs[:, None], normed_local, kv_all, cosine, sine, q_pieces, i, attended)
    context, query, lse = attended
    middle, *normed_mid_local = out_proj(context, tokens_here, gain_mlp, out_pieces)
    normed_mid = [over_tensor(x) for x in normed_mid_local]
    d_hidden, *cot_all = d_hidden_of(me_z.reshape(1), cots, down_pieces)
    hidden, mlp_grads, d_normed_mid, mlp_branch = [], [], [], []
    for i in range(2):
        h, g = mlp(normed_mid[i], d_hidden, i, gu_pieces)
        hidden.append(h[None])
        mlp_grads.append(g)
        d_normed_mid.append(sum_tensor(back(g, gu_pieces)))
        mlp_branch.append(sum_tensor(back(h[None], down_pieces)))
    _, cuts = scatter_segments(n_dp)
    half = [WIDTH // 2]

    def scattered(lefts, rights, which=0):
        other = weight_grad(lefts, rights, which, 1, None, half)[0]
        got = swap(other, DP, n_dp, 0)
        return dp_scatter(weight_grad(lefts, rights, which, 0, got, cuts), n_dp)

    down_parts = scattered(cot_all, hidden)
    gate_parts = scattered(normed_mid, mlp_grads, 0)
    up_parts = scattered(normed_mid, mlp_grads, 1)

    d_middle, d_branch, mlp_gain_part = mid_back(d_normed_mid, middle, gain_mlp, cot_here)
    dq, d_kv, d_normed_part = attn_backward(
        row0, own_segs[None, :], query, kv_all, d_branch, context, lse, cosine, sine, all_cosine, all_sine, q_pieces, out_pieces
    )
    d_kv = sum_tensor(d_kv)
    out_parts = scattered([d_branch], [context[None]])
    query_parts = scattered([normed_local], [dq[None]])
    kv_parts = scattered([normed_local], [d_kv[None]])
    input_grad, gain_parts = in_back(
        order, d_kv, d_normed_part, tokens_here, gain_attn, d_middle, mlp_gain_part, kv_pieces
    )

    grad_down = finish(down_parts, ff, 1, ways, True)[0]
    grad_gate = finish(gate_parts, ff, 1, ways, False)[0]
    grad_up = finish(up_parts, ff, 1, ways, False)[0]
    shard_rows = WIDTH // n_dp
    pair = LANES // kv if kv < LANES else 1
    kv_at = [z // pair * 2 * max(kv, LANES) + z % pair * kv for z in range(n_tensor)]
    q_at = [z * q for z in range(n_tensor)]
    packed = pack([query_parts, out_parts], [[(0, q, q_at)], [(q, q, q_at)]], n_tensor, ways, 2 * q, shard_rows)
    packed = sum_tensor(packed).astype(f32)
    grad_query, grad_output = packed[:, :q], packed[:, q:].T
    kv_cuts = [(0, kv, kv_at), (kv, kv, [x + max(kv, LANES) for x in kv_at])]
    packed = sum_tensor(pack([kv_parts], [kv_cuts], n_tensor, ways, 2 * kv, shard_rows)).astype(f32)
    grad_key, grad_value = packed[:, :kv], packed[:, kv:]

    def sum_all(x):
        for b in range(n_tensor.bit_length() - 1):
            x = x + swap(x, TENSOR, n_tensor, b)
        for b in range(n_dp.bit_length() - 1):
            x = x + swap(x, DP, n_dp, b)
        return x

    layer_out = (middle + jnp.concatenate(mlp_branch, axis=0).astype(f32)).astype(bf16)
    layer_out = reorder(order, (layer_out,), True)[0]
    gain_grads = sum_all(gain_parts)
    return (
        layer_out, input_grad, gain_grads[0], grad_query, grad_key, grad_value, grad_output,
        gain_grads[1], grad_gate, grad_up, grad_down,
    )


def solution(mesh):
    sizes = dict(mesh.shape)
    in_specs = (
        P((DP, TENSOR), None),
        P(DP),
        P(DP),
        P(),
        P(DP, TENSOR),
        P(DP, TENSOR),
        P(DP, TENSOR),
        P(TENSOR, DP),
        P(),
        P(DP, TENSOR),
        P(DP, TENSOR),
        P(TENSOR, DP),
        P((DP, TENSOR), None),
    )
    out_specs = (
        P((DP, TENSOR), None),
        P((DP, TENSOR), None),
        P(),
        P(DP, TENSOR),
        P(DP, TENSOR),
        P(DP, TENSOR),
        P(TENSOR, DP),
        P(),
        P(DP, TENSOR),
        P(DP, TENSOR),
        P(TENSOR, DP),
    )
    body = partial(layer, n_dp=sizes[DP], n_tensor=sizes[TENSOR])
    return jax.shard_map(body, mesh=mesh, in_specs=in_specs, out_specs=out_specs, check_vma=False)
```

```python
from functools import partial
import math

import jax
import jax.numpy as jnp
from jax import lax
from jax.experimental import pallas as pl
from jax.experimental.pallas import tpu as pltpu
from jax.sharding import PartitionSpec as P


QH = 32
KVH = 8
HD = 64
LEN = 1024
WIDTH = 2048
GROUP = QH // KVH
LANES = 128
TILE = 2 * LANES
ROW_STEP = 64
NEG = -1e30
DP, TENSOR = "dp", "tensor"
EPS = 1e-05
VMEM_LIMIT = 58 << 20


f32 = jnp.float32
bf16 = jnp.bfloat16


def dot(a, b, contract):
    return lax.dot_general(a, b, (contract, ((), ())), preferred_element_type=f32)


def ways_of(n):
    return 2 if WIDTH // n >= 2 * LANES else 1


def routes_of(n):
    bits = list(range(1, n.bit_length() - 1))
    return [bits, bits[::-1]][: ways_of(n)]


def block_slots(n):
    count, ways = n // 2, ways_of(n)
    return [(h, 0) for h in range(ways)] + [(h, s) for h in range(ways) for s in range(1, count)]


def width_order(n):
    routes, ways = routes_of(n), ways_of(n)
    order = []
    for core in range(2):
        for h, s in block_slots(n):
            j = core
            for t, b in enumerate(routes[h]):
                j |= ((s >> t) & 1) << b
            order.append(ways * j + h)
    return order


def swap(x, axis, n, b):
    return lax.ppermute(x, axis, [(i, i ^ (1 << b)) for i in range(n)])


def dp_gather(shard, n, cut=None):
    routes, ways = routes_of(n), ways_of(n)
    size = shard.shape[0] // ways
    parts = [[cut[h] if cut else shard[h * size : (h + 1) * size]] for h in range(ways)]
    for t in range(len(routes[0])):
        for h in range(ways):
            parts[h] += [swap(p, DP, n, routes[h][t]) for p in parts[h]]
    own = [shard] + [p for part in parts for p in part[1:]]
    return own + [swap(p, DP, n, 0) for p in own]


def scatter_segments(n):
    count, ways = n // 2, ways_of(n)
    size = WIDTH // n // ways
    half = count // 2
    cuts = [(ways + half - 1) * size, half * size]
    if ways > 1:
        cuts += [(half - 1) * size, half * size]
    return size, cuts


def add_kernel(*refs, spans):
    count = len(spans)
    for i, (at, rows, size) in enumerate(spans):
        kept, got, out = refs[2 * i], refs[2 * i + 1], refs[2 * count + i]
        total = kept[pl.ds(at, rows), :].astype(f32) + got[pl.ds(size, rows), :].astype(f32)
        out[...] = total.astype(bf16)


def add_rows(pairs, size):
    tile = 1024
    columns = pairs[0][0].shape[1]
    arrays = [x for array, _, _, got in pairs for x in (array, got)]
    return pl.pallas_call(
        partial(add_kernel, spans=[(at, rows, size) for _, at, rows, _ in pairs]),
        grid=(columns // tile,),
        in_specs=[pl.BlockSpec((x.shape[0], tile), lambda i: (0, i)) for x in arrays],
        out_specs=tuple(pl.BlockSpec((rows, tile), lambda i: (0, i)) for _, _, rows, _ in pairs),
        out_shape=tuple(jax.ShapeDtypeStruct((rows, columns), bf16) for _, _, rows, _ in pairs),
        compiler_params=pltpu.CompilerParams(vmem_limit_bytes=VMEM_LIMIT),
    )(*arrays)


def dp_scatter(pieces, n):
    routes, ways = routes_of(n), ways_of(n)
    size, _ = scatter_segments(n)
    kept = [(pieces[0], ways * size)] + ([(pieces[2], 0)] if ways > 1 else [])
    send = [pieces[1]] + ([pieces[3]] if ways > 1 else [])
    terms = [[] for _ in range(ways)]
    slots = n // 4
    for t in reversed(range(len(routes[0]))):
        for h in range(ways):
            terms[h].append(swap(send[h], DP, n, routes[h][t]))
        if t:
            rows = (slots - 1) * size
            sums = add_rows([(*kept[h], rows, terms[h][-1]) for h in range(ways)], size)
            slots //= 2
            send = [x[(slots - 1) * size :] if slots > 1 else x for x in sums]
            kept = [(x, 0) for x in sums]
    return pieces[0], terms


def width_at(order_ref, k, width):
    return pl.ds(pl.multiple_of(order_ref[k] * width, width), width)


def reorder_kernel(order_ref, *refs, inverse):
    ins, outs = refs[: len(refs) // 2], refs[len(refs) // 2 :]
    count = order_ref.shape[0]
    for src, dst in zip(ins, outs):
        width = src.shape[1] // count
        for k in range(count):
            here = pl.ds(k * width, width)
            if inverse:
                dst[:, width_at(order_ref, k, width)] = src[:, here]
            else:
                dst[:, here] = src[:, width_at(order_ref, k, width)]


SMEM_SPEC = pl.BlockSpec(memory_space=pltpu.SMEM)
VMEM_SPEC = pl.BlockSpec(memory_space=pltpu.VMEM)


def reorder(order, arrays, inverse):
    return pl.pallas_call(
        partial(reorder_kernel, inverse=inverse),
        out_shape=tuple(jax.ShapeDtypeStruct(a.shape, a.dtype) for a in arrays),
        in_specs=[SMEM_SPEC] + [VMEM_SPEC] * len(arrays),
        out_specs=tuple(VMEM_SPEC for _ in arrays),
    )(order, *arrays)


def rows_loop(count, body):
    step = min(ROW_STEP, count)

    def one(r, _):
        body(pl.ds(pl.multiple_of(r * step, step), step))
        return 0

    lax.fori_loop(0, count // step, one, 0)


def enter_kernel(order_ref, tok_ref, cot_ref, gain1_ref, gain2_ref, tok_out, cot_out, gain1_out, gain2_out, norm_ref):
    count = order_ref.shape[0]
    width = tok_ref.shape[1] // count
    for src, dst in ((tok_ref, tok_out), (cot_ref, cot_out), (gain1_ref, gain1_out), (gain2_ref, gain2_out)):
        for k in range(count):
            dst[:, k * width : (k + 1) * width] = src[:, width_at(order_ref, k, width)]

    def normalize(at):
        values = tok_out[at, :].astype(f32)
        inverse = lax.rsqrt(jnp.mean(values * values, axis=1, keepdims=True) + EPS)
        norm_ref[at, :] = (values * inverse * gain1_out[...]).astype(bf16)

    rows_loop(tok_ref.shape[0], normalize)


def enter(order, tokens, cotangent, gain1, gain2):
    arrays = (tokens, cotangent, gain1, gain2)
    return pl.pallas_call(
        enter_kernel,
        out_shape=tuple(jax.ShapeDtypeStruct(a.shape, a.dtype) for a in (*arrays, tokens)),
        in_specs=[SMEM_SPEC] + [VMEM_SPEC] * 4,
        out_specs=tuple(VMEM_SPEC for _ in range(5)),
        name="ro",
    )(order, *arrays)


def unpack_kernel(me_ref, *refs, groups, counts):
    ins, outs = refs[:counts], refs[counts:]
    per = len(outs) // groups
    rows = outs[0].shape[0]
    cuts = [x[pl.ds(k * rows, rows), :] for x in ins for k in range(x.shape[0] // rows)]
    for s, cut in enumerate(cuts):
        for i in range(groups):
            mine = outs[i * per : (i + 1) * per]
            width = cut.shape[1] // groups
            value = cut[:, i * width : (i + 1) * width]
            if counts > 1:
                z = jnp.bitwise_xor(me_ref[0], s)
                at = pl.ds(pl.multiple_of(z * width, width), width)
            else:
                at = pl.ds(s * width, width)
            mine[0][:, at] = value
            size = rows // max(1, per - 1)
            for h in range(per - 1):
                mine[h + 1][:, at] = value[h * size : (h + 1) * size]


def unpack(me, cuts, groups, n_tensor, ways):
    rows = sum(x.shape[0] for x in cuts) // n_tensor
    columns = cuts[0].shape[1] // groups * n_tensor
    shapes = [(rows, columns)] + [(rows // ways, columns)] * ways
    outs = pl.pallas_call(
        partial(unpack_kernel, groups=groups, counts=len(cuts)),
        out_shape=tuple(jax.ShapeDtypeStruct(x, bf16) for x in shapes * groups),
        in_specs=[SMEM_SPEC] + [VMEM_SPEC] * len(cuts),
        out_specs=tuple(VMEM_SPEC for _ in shapes * groups),
    )(me, *cuts)
    per = len(shapes)
    return [(outs[i * per], outs[i * per + 1 : (i + 1) * per]) for i in range(groups)]


def shard_sum(first_ref, terms, ways, at):
    parts = []
    for h in range(ways):
        size = terms[h][-1].shape[0]
        total = first_ref[pl.ds(h * size, size), at].astype(f32)
        for t in terms[h]:
            total = total + t[pl.ds(0, size), at].astype(f32)
        parts.append(total)
    return parts[0] if ways == 1 else jnp.concatenate(parts, axis=0)


def transpose_kernel(in_ref, out_ref, *parts):
    value = in_ref[...].T
    out_ref[...] = value
    for h, part in enumerate(parts):
        part[...] = value[h * part.shape[0] : (h + 1) * part.shape[0]]


def beside_kernel(left_ref, right_ref, out_ref):
    columns = left_ref.shape[1]
    out_ref[:, :columns] = left_ref[...]
    out_ref[:, columns:] = right_ref[...].T


def beside(left, right):
    return pl.pallas_call(
        beside_kernel,
        out_shape=jax.ShapeDtypeStruct((left.shape[0], left.shape[1] + right.shape[0]), left.dtype),
        in_specs=[VMEM_SPEC, VMEM_SPEC],
        out_specs=VMEM_SPEC,
        name="cq",
    )(left, right)


def transposed(x, ways):
    columns, rows = x.shape
    shapes = [(rows, columns)] + [(rows // ways, columns)] * ways
    out, *parts = pl.pallas_call(
        transpose_kernel,
        out_shape=tuple(jax.ShapeDtypeStruct(y, x.dtype) for y in shapes),
        in_specs=[VMEM_SPEC],
        out_specs=tuple(VMEM_SPEC for _ in shapes),
    )(x)
    return out, parts


def split_terms(refs, ways):
    each = len(refs) // ways
    return [refs[h * each : (h + 1) * each] for h in range(ways)]


def flat(scattered):
    first, terms = scattered
    return [first] + [t for part in terms for t in part]


def pack_kernel(*refs, n_tensor, ways, groups):
    out_ref = refs[-1]
    rows = out_ref.shape[0] // n_tensor
    count = (len(refs) - 1) // len(groups)
    for i, cuts in enumerate(groups):
        mine = refs[i * count : (i + 1) * count]
        terms = split_terms(mine[1:], ways)
        for at, width, starts in cuts:
            for z in range(n_tensor):
                total = shard_sum(mine[0], terms, ways, pl.ds(starts[z], width))
                out_ref[pl.ds(z * rows, rows), pl.ds(at, width)] = total.astype(out_ref.dtype)


def pack(scattered, groups, n_tensor, ways, columns, rows):
    arrays = [a for s in scattered for a in flat(s)]
    return pl.pallas_call(
        partial(pack_kernel, n_tensor=n_tensor, ways=ways, groups=groups),
        out_shape=jax.ShapeDtypeStruct((n_tensor * rows, columns), bf16),
        in_specs=[VMEM_SPEC] * len(arrays),
        out_specs=VMEM_SPEC,
        compiler_params=pltpu.CompilerParams(vmem_limit_bytes=VMEM_LIMIT),
    )(*arrays)


def final_kernel(*refs, ways, outs, transposed):
    outputs = refs[-outs:]
    refs = refs[:-outs]
    total = shard_sum(refs[0], split_terms(refs[1:], ways), ways, slice(None))
    total = total.T if transposed else total
    each = pl.num_programs(0) // outs
    for k, out in enumerate(outputs):

        @pl.when(pl.program_id(0) // each == k)
        def _(out=out):
            out[...] = total


def finish(scattered, columns, outs, ways, transposed):
    arrays = flat(scattered)
    size = scattered[1][0][-1].shape[0]
    rows = ways * size
    tile = 512
    each = columns // tile
    blocks = [rows] + [size] * (len(arrays) - 1)
    at = [partial(lambda i, k: jnp.clip(i - k * each, 0, each - 1), k=k) for k in range(outs)]
    specs = [
        pl.BlockSpec((tile, rows), partial(lambda i, f: (f(i), 0), f=f))
        if transposed
        else pl.BlockSpec((rows, tile), partial(lambda i, f: (0, f(i)), f=f))
        for f in at
    ]
    return pl.pallas_call(
        partial(final_kernel, ways=ways, outs=outs, transposed=transposed),
        grid=(outs * each,),
        out_shape=tuple(jax.ShapeDtypeStruct((columns, rows) if transposed else (rows, columns), f32) for _ in at),
        in_specs=[pl.BlockSpec((b, tile), lambda i: (0, i)) for b in blocks],
        out_specs=tuple(specs),
    )(*arrays)


def joined(refs):
    return jnp.concatenate([r[...] for r in refs], axis=0)


def piece_specs(pieces, tile, column):
    return [pl.BlockSpec((p.shape[0], tile), lambda i, *_: (0, column(i))) for p in pieces]


def tables_kernel(row0_ref, cos_ref, sin_ref, all_cos_ref, all_sin_ref, own_cos_ref, own_sin_ref):
    repeat = LANES // cos_ref.shape[1]
    cosine, sine = cos_ref[...], sin_ref[...]
    all_cos_ref[...] = jnp.concatenate([cosine] * repeat, axis=1)
    all_sin_ref[...] = jnp.concatenate([-sine, sine] * (repeat // 2), axis=1)
    own = pl.ds(pl.multiple_of(row0_ref[0], own_cos_ref.shape[0]), own_cos_ref.shape[0])
    own_cos_ref[...] = all_cos_ref[own, :]
    own_sin_ref[...] = all_sin_ref[own, :]


def rotary_tables(row0, cosine, sine, rows):
    shapes = [(cosine.shape[0], LANES)] * 2 + [(rows, LANES)] * 2
    return pl.pallas_call(
        tables_kernel,
        out_shape=tuple(jax.ShapeDtypeStruct(x, f32) for x in shapes),
        in_specs=[SMEM_SPEC, VMEM_SPEC, VMEM_SPEC],
        out_specs=tuple(VMEM_SPEC for _ in shapes),
        name="tb",
    )(row0, cosine, sine)


def swap_halves(u):
    lane = lax.broadcasted_iota(jnp.int32, u.shape, 1)
    up = pltpu.roll(u, HD // 2, 1)
    down = pltpu.roll(u, LANES - HD // 2, 1)
    return jnp.where((lane % HD) < HD // 2, down, up)


def turn(u, cosine, signed_sine, back):
    s = swap_halves(u) * signed_sine
    return u * cosine - s if back else u * cosine + s


def proj_kv_kernel(x_ref, cos_ref, sin_ref, *refs):
    out_ref = refs[-1]
    raw = dot(x_ref[...], joined(refs[:-1]), ((1,), (0,)))
    out_ref[:, :LANES] = turn(raw[:, :LANES], cos_ref[...], sin_ref[...], False).astype(bf16)
    out_ref[:, LANES:] = raw[:, LANES:].astype(bf16)


def proj_kv(x, cosine, sine, pieces):
    rows = x.shape[0]
    whole = lambda shape: pl.BlockSpec(shape, lambda i: (0, 0))
    return pl.pallas_call(
        proj_kv_kernel,
        grid=(2 * KVH * HD // TILE,),
        in_specs=[whole(x.shape), whole(cosine.shape), whole(sine.shape)] + piece_specs(pieces, TILE, lambda i: i),
        out_specs=pl.BlockSpec((rows, TILE), lambda i: (0, i)),
        out_shape=jax.ShapeDtypeStruct((rows, 2 * KVH * HD), bf16),
        cost_estimate=pl.CostEstimate(flops=4 * rows * WIDTH * KVH * HD, bytes_accessed=6 << 20, transcendentals=0),
        compiler_params=pltpu.CompilerParams(vmem_limit_bytes=VMEM_LIMIT),
        name="pk",
    )(x, cosine, sine, *pieces)


def split_halves(block, odd):
    wide = block.astype(f32)
    rolled = pltpu.roll(wide, HD, 1)
    lane = lax.broadcasted_iota(jnp.int32, wide.shape, 1)
    low = lane < HD
    first = jnp.where(odd, rolled, wide)
    second = jnp.where(odd, wide, rolled)
    zero = jnp.zeros_like(wide)
    return jnp.where(low, first, zero).astype(bf16), jnp.where(low, zero, second).astype(bf16)


def attn_fwd_kernel(row0_ref, seg_ref, x_ref, k_ref, v_ref, cos_ref, sin_ref, *refs, count):
    w_query = refs[:count]
    ctx_ref, rot_ref, lse_ref, bias_ref = refs[-4:]
    g = pl.program_id(0)
    rows = x_ref.shape[0]

    @pl.when(g == 0)
    def _():
        t = row0_ref[0] + lax.broadcasted_iota(jnp.int32, bias_ref.shape, 0)
        s = lax.broadcasted_iota(jnp.int32, bias_ref.shape, 1)
        allowed = (s <= t) & (s >= seg_ref[...])
        bias_ref[...] = jnp.where(allowed, 0.0, NEG)

    q_raw = dot(x_ref[...], joined(w_query), ((1,), (0,)))
    odd = lax.rem(g, 2) == 1
    keys = split_halves(k_ref[...], odd)
    values = split_halves(v_ref[...], odd)
    lane = lax.broadcasted_iota(jnp.int32, (rows, LANES), 1)
    log_sums = jnp.zeros((rows, LANES), f32)
    for c in range(GROUP // 2):
        at = pl.ds(c * LANES, LANES)
        turned = turn(q_raw[:, c * LANES : (c + 1) * LANES], cos_ref[...], sin_ref[...], False)
        query = (turned * (HD**-0.5)).astype(bf16)
        rot_ref[:, at] = query
        total = jnp.zeros((rows, LANES), f32)
        for e in range(2):
            scores = dot(query, keys[e], ((1,), (1,))) + bias_ref[...]
            peak = jnp.max(scores, axis=1, keepdims=True)
            weights = jnp.exp(scores - peak)
            mass = jnp.sum(weights, axis=1, keepdims=True)
            part = dot(weights.astype(bf16), values[e], ((1,), (0,)))
            total = total + part * (1.0 / mass)
            log_sums = jnp.where(lane == 2 * c + e, peak + jnp.log(mass), log_sums)
        ctx_ref[:, at] = total.astype(bf16)
    lse_ref[...] = log_sums


FWD_PARTS = 2


def attn_forward(row0, seg_col, x, kv, cosine, sine, pieces, part, before):
    rows = x.shape[0]
    heads = KVH // FWD_PARTS
    base = part * heads
    args = [row0, seg_col, x, kv, kv, cosine, sine, *pieces]
    whole = lambda shape: pl.BlockSpec(shape, lambda g, r: (0, 0))
    grid_spec = pltpu.PrefetchScalarGridSpec(
        num_scalar_prefetch=1,
        grid=(heads,),
        in_specs=[
            whole((rows, 1)),
            whole(x.shape),
            pl.BlockSpec((LEN, LANES), lambda g, r: (0, (base + g) // 2 * 2)),
            pl.BlockSpec((LEN, LANES), lambda g, r: (0, (base + g) // 2 * 2 + 1)),
            whole((rows, LANES)),
            whole((rows, LANES)),
        ]
        + piece_specs(pieces, TILE, lambda g: base + g)
        + [pl.BlockSpec(memory_space=pl.ANY)] * len(before),
        out_specs=[
            pl.BlockSpec((rows, TILE), lambda g, r: (0, base + g)),
            pl.BlockSpec((rows, TILE), lambda g, r: (0, base + g)),
            pl.BlockSpec((rows, LANES), lambda g, r: (0, base + g)),
        ],
        scratch_shapes=[pltpu.VMEM((rows, LEN), f32)],
    )
    return pl.pallas_call(
        partial(attn_fwd_kernel, count=len(pieces)),
        grid_spec=grid_spec,
        out_shape=(
            jax.ShapeDtypeStruct((rows, QH * HD), bf16),
            jax.ShapeDtypeStruct((rows, QH * HD), bf16),
            jax.ShapeDtypeStruct((rows, KVH * LANES), f32),
        ),
        cost_estimate=pl.CostEstimate(
            flops=8 * rows * LEN * QH * HD, bytes_accessed=12 << 20, transcendentals=rows * LEN * QH // FWD_PARTS
        ),
        compiler_params=pltpu.CompilerParams(vmem_limit_bytes=VMEM_LIMIT),
        input_output_aliases={len(args) + i: i for i in range(len(before))},
    )(*args, *before)


def out_proj_kernel(ctx_ref, tok_ref, gain_ref, *refs):
    mid_ref, first_ref, second_ref, sum_ref = refs[-4:]
    i = pl.program_id(0)

    @pl.when(i == 0)
    def _():
        sum_ref[...] = tok_ref[...].astype(f32)

    sum_ref[...] += dot(ctx_ref[...], joined(refs[:-4]), ((1,), (1,)))

    @pl.when(i == pl.num_programs(0) - 1)
    def _():
        half = first_ref.shape[0]
        step = min(ROW_STEP, half)

        for k, out_ref in enumerate((first_ref, second_ref)):

            def body(r, _, k=k, out_ref=out_ref):
                at = pl.ds(pl.multiple_of(k * half + r * step, step), step)
                middle = sum_ref[at, :]
                mid_ref[at, :] = middle
                inverse = lax.rsqrt(jnp.mean(middle * middle, axis=1, keepdims=True) + EPS)
                out_ref[pl.ds(pl.multiple_of(r * step, step), step), :] = (middle * inverse * gain_ref[...]).astype(bf16)
                return 0

            lax.fori_loop(0, half // step, body, 0)


def out_proj(context, tokens, gain, pieces):
    rows = context.shape[0]
    tile = 512
    whole = lambda shape: pl.BlockSpec(shape, lambda i: (0, 0))
    return pl.pallas_call(
        out_proj_kernel,
        grid=(QH * HD // tile,),
        in_specs=[pl.BlockSpec((rows, tile), lambda i: (0, i)), whole(tokens.shape), whole(gain.shape)]
        + piece_specs(pieces, tile, lambda i: i),
        out_specs=(whole((rows, WIDTH)), whole((rows // 2, WIDTH)), whole((rows // 2, WIDTH))),
        out_shape=(
            jax.ShapeDtypeStruct((rows, WIDTH), f32),
            jax.ShapeDtypeStruct((rows // 2, WIDTH), bf16),
            jax.ShapeDtypeStruct((rows // 2, WIDTH), bf16),
        ),
        scratch_shapes=[pltpu.VMEM((rows, WIDTH), f32)],
        cost_estimate=pl.CostEstimate(flops=2 * rows * WIDTH * QH * HD, bytes_accessed=14 << 20, transcendentals=0),
        compiler_params=pltpu.CompilerParams(vmem_limit_bytes=VMEM_LIMIT),
        name="op",
    )(context, tokens, gain, *pieces)


def rms_back(values, gain, grad):
    inverse = lax.rsqrt(jnp.mean(values * values, axis=1, keepdims=True) + EPS)
    scaled = gain * grad
    along = jnp.mean(scaled * values, axis=1, keepdims=True)
    d_values = inverse * scaled - values * (inverse * inverse * inverse) * along
    d_gain = jnp.sum(grad * values * inverse, axis=0, keepdims=True)
    return d_values, d_gain


def mid_back_kernel(mid_ref, gain_ref, cot_ref, *refs):
    dmid_ref, db_ref, dg_ref = refs[-3:]
    each = refs[0].shape[0]
    step = min(ROW_STEP, each)
    dg_ref[...] = jnp.zeros_like(dg_ref)

    for k, dn_ref in enumerate(refs[:-3]):

        def body(r, _, k=k, dn_ref=dn_ref):
            at = pl.ds(pl.multiple_of(k * each + r * step, step), step)
            grad = dn_ref[pl.ds(pl.multiple_of(r * step, step), step), :].astype(f32)
            d_values, d_gain = rms_back(mid_ref[at, :], gain_ref[...], grad)
            d_middle = cot_ref[at, :].astype(f32) + d_values
            dmid_ref[at, :] = d_middle
            db_ref[at, :] = d_middle.astype(bf16)
            dg_ref[0:1, :] += d_gain
            return 0

        lax.fori_loop(0, each // step, body, 0)


def mid_back(d_normed, middle, gain, cot):
    rows = middle.shape[0]
    return pl.pallas_call(
        mid_back_kernel,
        out_shape=(
            jax.ShapeDtypeStruct((rows, WIDTH), f32),
            jax.ShapeDtypeStruct((rows, WIDTH), bf16),
            jax.ShapeDtypeStruct((8, WIDTH), f32),
        ),
        name="mb",
    )(middle, gain, cot, *d_normed)


def attn_bwd_kernel(
    row0_ref, seg_ref, q_ref, k_ref, v_ref, db_ref, ctx_ref, lse_ref, cos_ref, sin_ref, all_cos_ref, all_sin_ref, *refs, count
):
    w_query, w_out = refs[:count], refs[count : 2 * count]
    dq_ref, dkv_ref, dn_ref, bias_ref = refs[2 * count :]
    g = pl.program_id(0)
    rows = q_ref.shape[0]

    @pl.when(g == 0)
    def _():
        s = lax.broadcasted_iota(jnp.int32, bias_ref.shape, 0)
        t = row0_ref[0] + lax.broadcasted_iota(jnp.int32, bias_ref.shape, 1)
        allowed = (s <= t) & (s >= seg_ref[...])
        bias_ref[...] = jnp.where(allowed, 0.0, NEG)
        dn_ref[...] = jnp.zeros_like(dn_ref)

    d_context = dot(db_ref[...], joined(w_out), ((1,), (0,))).astype(bf16)
    odd = lax.rem(g, 2) == 1
    keys = split_halves(k_ref[...], odd)
    values = split_halves(v_ref[...], odd)
    log_sums = lse_ref[...].T
    low = lax.broadcasted_iota(jnp.int32, (rows, LANES), 1) < HD
    dk_sum = jnp.zeros((LEN, LANES), f32)
    dv_sum = jnp.zeros((LEN, LANES), f32)
    for c in range(GROUP // 2):
        at = pl.ds(c * LANES, LANES)
        query, d_rows = q_ref[:, at], d_context[:, c * LANES : (c + 1) * LANES]
        both = (d_rows.astype(f32) * ctx_ref[:, at].astype(f32)).T
        dq = jnp.zeros((rows, LANES), f32)
        for e in range(2):
            mine = low if e == 0 else jnp.logical_not(low)
            delta = jnp.sum(both[e * HD : (e + 1) * HD], axis=0, keepdims=True)
            h = 2 * c + e
            scores = dot(keys[e], query, ((1,), (1,))) + bias_ref[...]
            probs = jnp.exp(scores - log_sums[h : h + 1])
            d_probs = dot(values[e], d_rows, ((1,), (1,)))
            d_scores = (probs * (d_probs - delta)).astype(bf16)
            zero = jnp.zeros_like(query)
            dv_sum = dv_sum + dot(probs.astype(bf16), jnp.where(mine, d_rows, zero), ((1,), (0,)))
            dk_sum = dk_sum + dot(d_scores, jnp.where(mine, query, zero), ((1,), (0,)))
            dq = dq + dot(d_scores, keys[e], ((0,), (0,)))
        dq_ref[:, at] = turn(dq * (HD**-0.5), cos_ref[...], sin_ref[...], True).astype(bf16)
    dn_ref[...] += dot(dq_ref[...], joined(w_query), ((1,), (1,)))
    wide_low = lax.broadcasted_iota(jnp.int32, (LEN, LANES), 1) < HD
    keep = wide_low == odd
    dk_sum = turn(dk_sum + pltpu.roll(dk_sum, HD, 1), all_cos_ref[...], all_sin_ref[...], True)
    dv_sum = dv_sum + pltpu.roll(dv_sum, HD, 1)
    for i, total in enumerate((dk_sum, dv_sum)):
        at = pl.ds(i * LANES, LANES)
        dkv_ref[:, at] = jnp.where(keep, dkv_ref[:, at], total.astype(bf16))


def attn_backward(row0, seg_row, query, kv, d_branch, context, lse, cosine, sine, all_cosine, all_sine, q_pieces, out_pieces):
    rows = query.shape[0]
    whole = lambda shape: pl.BlockSpec(shape, lambda g, r: (0, 0))
    grid_spec = pltpu.PrefetchScalarGridSpec(
        num_scalar_prefetch=1,
        grid=(KVH,),
        in_specs=[
            whole((1, rows)),
            pl.BlockSpec((rows, TILE), lambda g, r: (0, g)),
            pl.BlockSpec((LEN, LANES), lambda g, r: (0, g // 2 * 2)),
            pl.BlockSpec((LEN, LANES), lambda g, r: (0, g // 2 * 2 + 1)),
            whole((rows, WIDTH)),
            pl.BlockSpec((rows, TILE), lambda g, r: (0, g)),
            pl.BlockSpec((rows, LANES), lambda g, r: (0, g)),
            whole((rows, LANES)),
            whole((rows, LANES)),
            whole((LEN, LANES)),
            whole((LEN, LANES)),
        ]
        + piece_specs(q_pieces, TILE, lambda g: g)
        + piece_specs(out_pieces, TILE, lambda g: g),
        out_specs=[
            pl.BlockSpec((rows, TILE), lambda g, r: (0, g)),
            pl.BlockSpec((LEN, TILE), lambda g, r: (0, g // 2)),
            whole((rows, WIDTH)),
        ],
        scratch_shapes=[pltpu.VMEM((LEN, rows), f32)],
    )
    return pl.pallas_call(
        partial(attn_bwd_kernel, count=len(q_pieces)),
        grid_spec=grid_spec,
        out_shape=(
            jax.ShapeDtypeStruct((rows, QH * HD), bf16),
            jax.ShapeDtypeStruct((LEN, 2 * KVH * HD), bf16),
            jax.ShapeDtypeStruct((rows, WIDTH), f32),
        ),
        cost_estimate=pl.CostEstimate(
            flops=28 * rows * LEN * QH * HD, bytes_accessed=28 << 20, transcendentals=rows * LEN * QH
        ),
        compiler_params=pltpu.CompilerParams(vmem_limit_bytes=VMEM_LIMIT),
        name="ab",
    )(row0, seg_row, query, kv, kv, d_branch, context, lse, cosine, sine, all_cosine, all_sine, *q_pieces, *out_pieces)


def in_back_kernel(order_ref, dkv_ref, part_ref, tok_ref, gain_ref, dmid_ref, dg_mlp_ref, *refs):
    out_ref, dg_ref, sum_ref, gain_ref_sum = refs[-4:]
    i = pl.program_id(0)

    @pl.when(i == 0)
    def _():
        sum_ref[...] = part_ref[...]
        dg_ref[...] = jnp.zeros_like(dg_ref)

    sum_ref[...] += dot(dkv_ref[...], joined(refs[:-4]), ((1,), (1,)))

    @pl.when(i == pl.num_programs(0) - 1)
    def _():
        count = order_ref.shape[0]
        width = sum_ref.shape[1] // count
        gain_ref_sum[...] = jnp.zeros_like(gain_ref_sum)

        def body(at):
            d_values, d_gain = rms_back(tok_ref[at, :].astype(f32), gain_ref[...], sum_ref[at, :])
            d_values = d_values + dmid_ref[at, :]
            gain_ref_sum[0:1, :] += d_gain
            for k in range(count):
                out_ref[at, width_at(order_ref, k, width)] = d_values[:, k * width : (k + 1) * width]

        rows_loop(sum_ref.shape[0], body)
        for k in range(count):
            at = width_at(order_ref, k, width)
            here = pl.ds(k * width, width)
            dg_ref[0:1, at] = gain_ref_sum[0:1, here]
            dg_ref[1:2, at] = dg_mlp_ref[0:1, here]


def in_back(order, d_kv, part, tokens, gain, d_middle, mlp_gain, pieces):
    rows = tokens.shape[0]
    whole = lambda shape: pl.BlockSpec(shape, lambda i: (0, 0))
    return pl.pallas_call(
        in_back_kernel,
        grid=(2 * KVH * HD // TILE,),
        in_specs=[SMEM_SPEC, pl.BlockSpec((rows, TILE), lambda i: (0, i))]
        + [whole(a.shape) for a in (part, tokens, gain, d_middle, mlp_gain)]
        + piece_specs(pieces, TILE, lambda i: i),
        out_specs=(whole((rows, WIDTH)), whole((8, WIDTH))),
        out_shape=(jax.ShapeDtypeStruct((rows, WIDTH), f32), jax.ShapeDtypeStruct((8, WIDTH), f32)),
        scratch_shapes=[pltpu.VMEM((rows, WIDTH), f32), pltpu.VMEM((8, WIDTH), f32)],
        cost_estimate=pl.CostEstimate(flops=4 * rows * WIDTH * KVH * HD, bytes_accessed=16 << 20, transcendentals=0),
        compiler_params=pltpu.CompilerParams(vmem_limit_bytes=VMEM_LIMIT),
        name="ib",
    )(order, d_kv, part, tokens, gain, d_middle, mlp_gain, *pieces)


def d_hidden_kernel(me_ref, *refs, slots):
    cots, pieces = refs[: 2 * slots - 1], refs[2 * slots - 1 : -3]
    out_ref, first_ref, second_ref = refs[-3:]
    half = cots[0].shape[0] // 2

    @pl.when(pl.program_id(0) == 0)
    def _():
        for r in range(slots):
            z = lax.rem(me_ref[0] - r + slots, slots)
            at = pl.ds(pl.multiple_of(z * half, half), half)
            for k, whole_ref in enumerate((first_ref, second_ref)):
                here = pl.ds(k * half, half)
                value = cots[r][here, :] + cots[2 * slots - 1 - r][here, :] if r else cots[0][here, :]
                whole_ref[at, :] = value

    weights = joined(pieces)
    rows = first_ref.shape[0]
    out_ref[:rows, :] = dot(first_ref[...], weights, ((1,), (0,)))
    out_ref[rows:, :] = dot(second_ref[...], weights, ((1,), (0,)))


def d_hidden_of(me, cots, pieces):
    slots = (len(cots) + 1) // 2
    rows = cots[0].shape[0] * slots
    ff = pieces[0].shape[1]
    whole = lambda shape: pl.BlockSpec(shape, lambda i: (0, 0))
    half = (rows // 2, WIDTH)
    return pl.pallas_call(
        partial(d_hidden_kernel, slots=slots),
        grid=(ff // TILE,),
        in_specs=[SMEM_SPEC] + [whole(c.shape) for c in cots] + piece_specs(pieces, TILE, lambda i: i),
        out_specs=(pl.BlockSpec((rows, TILE), lambda i: (0, i)), whole(half), whole(half)),
        out_shape=(
            jax.ShapeDtypeStruct((rows, ff), f32),
            jax.ShapeDtypeStruct(half, bf16),
            jax.ShapeDtypeStruct(half, bf16),
        ),
        cost_estimate=pl.CostEstimate(flops=2 * rows * WIDTH * ff, bytes_accessed=24 << 20, transcendentals=0),
        compiler_params=pltpu.CompilerParams(vmem_limit_bytes=VMEM_LIMIT),
        name="dh",
    )(me, *cots, *pieces)


def mlp_kernel(x_ref, dh_ref, *refs, count):
    hidden_ref, grads_ref = refs[2 * count :]
    gate = dot(x_ref[...], joined(refs[:count]), ((1,), (0,)))
    up = dot(x_ref[...], joined(refs[count : 2 * count]), ((1,), (0,)))
    d_hidden = dh_ref[...]
    sig = jax.nn.sigmoid(gate)
    silu = gate * sig
    hidden_ref[...] = (silu * up).astype(bf16)
    grads_ref[0] = (d_hidden * up * (sig + silu * (1.0 - sig))).astype(bf16)
    grads_ref[1] = (d_hidden * silu).astype(bf16)


def mlp(x, d_hidden, chunk, pieces):
    rows = x.shape[0]
    ff = d_hidden.shape[1]
    tiles = ff // TILE
    specs = [pl.BlockSpec((rows, WIDTH), lambda i: (0, 0)), pl.BlockSpec((rows, TILE), lambda i: (chunk, i))]
    for base in (0, tiles):
        specs += piece_specs(pieces, TILE, partial(lambda i, base: base + i, base=base))
    return pl.pallas_call(
        partial(mlp_kernel, count=len(pieces)),
        grid=(tiles,),
        in_specs=specs,
        out_specs=(pl.BlockSpec((rows, TILE), lambda i: (0, i)), pl.BlockSpec((2, rows, TILE), lambda i: (0, 0, i))),
        out_shape=(jax.ShapeDtypeStruct((rows, ff), bf16), jax.ShapeDtypeStruct((2, rows, ff), bf16)),
        cost_estimate=pl.CostEstimate(flops=4 * rows * WIDTH * ff, bytes_accessed=30 << 20, transcendentals=rows * ff),
        compiler_params=pltpu.CompilerParams(vmem_limit_bytes=VMEM_LIMIT),
    )(x, d_hidden, *pieces, *pieces)


def back_kernel(x_ref, *refs, count):
    pieces, (out_ref, sum_ref) = refs[:count], refs[-2:]
    i = pl.program_id(0)
    rows = sum_ref.shape[0]

    @pl.when(i == 0)
    def _():
        def clear(at):
            sum_ref[at, :] = jnp.zeros((at.size, sum_ref.shape[1]), f32)

        rows_loop(rows, clear)

    sum_ref[...] += dot(x_ref[...].reshape(x_ref.shape[-2:]), joined(pieces), ((1,), (1,)))

    @pl.when(i == pl.num_programs(0) - 1)
    def _():
        each = rows // out_ref.shape[0]

        for z in range(out_ref.shape[0]):
            def write(at, z=z):
                out_ref[z, 0, at, :] = sum_ref[pl.ds(z * each + at.start, at.size), :].astype(bf16)

            rows_loop(each, write)


def back(x, pieces, n_tensor, chunk=0, chunks=1, before=()):
    many, rows, ff = x.shape
    tile = min(1024, ff)
    per = ff // tile
    each = rows // n_tensor
    out = pl.pallas_call(
        partial(back_kernel, count=len(pieces)),
        grid=(many * per,),
        in_specs=[pl.BlockSpec((1, rows, tile), lambda i: (i // per, 0, i % per))]
        + piece_specs(pieces, tile, lambda i: i)
        + [pl.BlockSpec(memory_space=pl.ANY)] * len(before),
        out_specs=pl.BlockSpec((n_tensor, 1, each, WIDTH), lambda i: (0, chunk, 0, 0)),
        out_shape=jax.ShapeDtypeStruct((n_tensor, chunks, each, WIDTH), bf16),
        scratch_shapes=[pltpu.VMEM((rows, WIDTH), f32)],
        cost_estimate=pl.CostEstimate(flops=2 * many * rows * WIDTH * ff, bytes_accessed=(12 << 20) * many, transcendentals=0),
        compiler_params=pltpu.CompilerParams(vmem_limit_bytes=VMEM_LIMIT),
        input_output_aliases={1 + len(pieces): 0} if before else {},
    )(x, *pieces, *before)
    return out


def grad_kernel(*refs, chunks, received, cuts):
    lefts, rights = refs[:chunks], refs[chunks : 2 * chunks]
    outs, turned_ref = refs[2 * chunks + received : -1], refs[-1]

    @pl.when(pl.program_id(0) == 0)
    def _():
        depth = lefts[0].shape[0]
        for c, left in enumerate(lefts):
            turned_ref[:, pl.ds(c * depth, depth)] = left[...].T

    right = jnp.concatenate([r[...].reshape(r.shape[-2:]) for r in rights], axis=0)
    total = dot(turned_ref[...], right, ((1,), (0,)))
    if received:
        total = total + refs[2 * chunks][...].astype(f32)
    at = 0
    for out, rows in zip(outs, cuts):
        out[...] = total[at : at + rows].astype(bf16)
        at += rows


def weight_grad(lefts, rights, which, block, got, cuts):
    _, depth, columns = rights[0].shape
    rows = WIDTH // 2
    tile = min(512, columns)
    chunks = len(lefts)
    column = lambda i: (0, i)
    extra = [got] if got is not None else []
    specs = [pl.BlockSpec((depth, rows), lambda i: (0, block))] * chunks
    specs += [pl.BlockSpec((1, depth, tile), lambda i: (which, 0, i))] * chunks
    specs += [pl.BlockSpec((rows, tile), column)] * len(extra)
    return pl.pallas_call(
        partial(grad_kernel, chunks=chunks, received=len(extra), cuts=cuts),
        grid=(columns // tile,),
        in_specs=specs,
        out_specs=tuple(pl.BlockSpec((c, tile), column) for c in cuts),
        out_shape=tuple(jax.ShapeDtypeStruct((c, columns), bf16) for c in cuts),
        scratch_shapes=[pltpu.VMEM((rows, depth * chunks), bf16)],
        cost_estimate=pl.CostEstimate(
            flops=2 * rows * depth * chunks * columns, bytes_accessed=8 * rows * columns, transcendentals=0
        ),
        compiler_params=pltpu.CompilerParams(vmem_limit_bytes=VMEM_LIMIT),
    )(*lefts, *rights, *extra)


def over_tensor(x, axis=0):
    return lax.all_gather(x, TENSOR, axis=axis, tiled=True)


def sum_tensor(x):
    return lax.psum_scatter(x, TENSOR, scatter_dimension=0, tiled=True)


def layer(
    tokens, segments, positions, norm_attn, w_query, w_key, w_value, w_out,
    norm_mlp, w_gate, w_up, w_down, cotangent, *, n_dp, n_tensor,
):
    me_dp, me_z = lax.axis_index(DP), lax.axis_index(TENSOR)
    rows, width = tokens.shape
    assert rows * n_tensor == LEN and width == WIDTH
    kv, q = w_key.shape[1], w_query.shape[1]
    ways = ways_of(n_dp)
    ff = w_gate.shape[1]
    order = jnp.bitwise_xor(jnp.array(width_order(n_dp), jnp.int32), ways * me_dp)
    row0 = (me_z * rows).reshape(1)
    own_segs = lax.dynamic_slice_in_dim(segments, me_z * rows, rows, 0)

    if kv % LANES == 0:
        slots = [jnp.concatenate([w_key, w_value], axis=1)]
        for b in range(n_tensor.bit_length() - 1):
            slots.append(swap(jnp.concatenate(slots, axis=0), TENSOR, n_tensor, b))
        kv_rows, kv_cut = unpack(me_z.reshape(1), slots, 1, n_tensor, ways)[0]
    else:
        pairs = [over_tensor(w, 1).reshape(w.shape[0], -1, LANES) for w in (w_key, w_value)]
        kv_rows, kv_cut = jnp.concatenate(pairs, axis=2).reshape(w_key.shape[0], -1), None
    kv_pieces = dp_gather(kv_rows, n_dp, kv_cut)
    both = over_tensor(beside(w_query, w_out))
    (q_rows, q_cut), (out_rows, out_cut) = unpack(me_z.reshape(1), [both], 2, n_tensor, ways)
    q_pieces = dp_gather(q_rows, n_dp, q_cut)
    out_pieces = dp_gather(out_rows, n_dp, out_cut)
    gu_pieces = dp_gather(jnp.concatenate([w_gate, w_up], axis=1), n_dp)
    down_rows, down_cut = transposed(w_down, ways)
    down_pieces = dp_gather(down_rows, n_dp, down_cut)

    tokens_here, cot_here, gain_attn, gain_mlp, normed_local = enter(
        order, tokens, cotangent, norm_attn[None], norm_mlp[None]
    )
    below, above = [cot_here], [cot_here]
    for r in range(1, n_tensor):
        below.append(lax.ppermute(below[-1], TENSOR, [(i, i + 1) for i in range(r - 1, n_tensor - 1)]))
        above.append(lax.ppermute(above[-1], TENSOR, [(i + 1, i) for i in range(n_tensor - r)]))
    cots = below + above[1:]

    freq_index = jnp.arange(HD // 2, dtype=jnp.int32).astype(f32)
    inverse = jnp.exp(freq_index * (-2.0 * math.log(500000.0) / HD))
    angles = positions.astype(f32)[:, None] * inverse[None, :]
    all_cosine, all_sine, cosine, sine = rotary_tables(row0, jnp.cos(angles), jnp.sin(angles), rows)

    kv_all = over_tensor(proj_kv(normed_local, cosine, sine, kv_pieces))
    attended = ()
    for i in range(FWD_PARTS):
        attended = attn_forward(row0, own_segs[:, None], normed_local, kv_all, cosine, sine, q_pieces, i, attended)
    context, query, lse = attended
    middle, *normed_mid_local = out_proj(context, tokens_here, gain_mlp, out_pieces)
    normed_mid = [over_tensor(x) for x in normed_mid_local]
    d_hidden, *cot_all = d_hidden_of(me_z.reshape(1), cots, down_pieces)
    hidden, mlp_grads, d_normed_mid, mlp_full = [], [], [], ()
    for i in range(2):
        h, g = mlp(normed_mid[i], d_hidden, i, gu_pieces)
        hidden.append(h[None])
        mlp_grads.append(g)
        d_normed_mid.append(sum_tensor(back(g, gu_pieces, n_tensor).reshape(LEN // 2, width)))
        mlp_full = (back(h[None], down_pieces, n_tensor, i, 2, mlp_full),)
    mlp_branch = sum_tensor(mlp_full[0].reshape(LEN, width))
    _, cuts = scatter_segments(n_dp)
    half = [WIDTH // 2]

    def scattered(lefts, rights, which=0):
        other = weight_grad(lefts, rights, which, 1, None, half)[0]
        got = swap(other, DP, n_dp, 0)
        return dp_scatter(weight_grad(lefts, rights, which, 0, got, cuts), n_dp)

    down_parts = scattered(cot_all, hidden)
    gate_parts = scattered(normed_mid, mlp_grads, 0)
    up_parts = scattered(normed_mid, mlp_grads, 1)

    d_middle, d_branch, mlp_gain_part = mid_back(d_normed_mid, middle, gain_mlp, cot_here)
    dq, d_kv, d_normed_part = attn_backward(
        row0, own_segs[None, :], query, kv_all, d_branch, context, lse, cosine, sine, all_cosine, all_sine, q_pieces, out_pieces
    )
    d_kv = sum_tensor(d_kv)
    out_parts = scattered([d_branch], [context[None]])
    query_parts = scattered([normed_local], [dq[None]])
    kv_parts = scattered([normed_local], [d_kv[None]])
    input_grad, gain_parts = in_back(
        order, d_kv, d_normed_part, tokens_here, gain_attn, d_middle, mlp_gain_part, kv_pieces
    )

    grad_down = finish(down_parts, ff, 1, ways, True)[0]
    grad_gate = finish(gate_parts, ff, 1, ways, False)[0]
    grad_up = finish(up_parts, ff, 1, ways, False)[0]
    shard_rows = WIDTH // n_dp
    pair = LANES // kv if kv < LANES else 1
    kv_at = [z // pair * 2 * max(kv, LANES) + z % pair * kv for z in range(n_tensor)]
    q_at = [z * q for z in range(n_tensor)]

    def over_all(parts, cuts, columns):
        packed = pack([parts], [cuts], n_tensor, ways, columns, shard_rows)
        return sum_tensor(packed).astype(f32)

    grad_output = over_all(out_parts, [(0, q, q_at)], q).T
    grad_query = over_all(query_parts, [(0, q, q_at)], q)
    kv_cuts = [(0, kv, kv_at), (kv, kv, [x + max(kv, LANES) for x in kv_at])]
    packed = over_all(kv_parts, kv_cuts, 2 * kv)
    grad_key, grad_value = packed[:, :kv], packed[:, kv:]

    def sum_all(x):
        for b in range(n_tensor.bit_length() - 1):
            x = x + swap(x, TENSOR, n_tensor, b)
        for b in range(n_dp.bit_length() - 1):
            x = x + swap(x, DP, n_dp, b)
        return x

    layer_out = (middle + mlp_branch.astype(f32)).astype(bf16)
    layer_out = reorder(order, (layer_out,), True)[0]
    gain_grads = sum_all(gain_parts)
    return (
        layer_out, input_grad, gain_grads[0], grad_query, grad_key, grad_value, grad_output,
        gain_grads[1], grad_gate, grad_up, grad_down,
    )


def solution(mesh):
    sizes = dict(mesh.shape)
    in_specs = (
        P((DP, TENSOR), None),
        P(DP),
        P(DP),
        P(),
        P(DP, TENSOR),
        P(DP, TENSOR),
        P(DP, TENSOR),
        P(TENSOR, DP),
        P(),
        P(DP, TENSOR),
        P(DP, TENSOR),
        P(TENSOR, DP),
        P((DP, TENSOR), None),
    )
    out_specs = (
        P((DP, TENSOR), None),
        P((DP, TENSOR), None),
        P(),
        P(DP, TENSOR),
        P(DP, TENSOR),
        P(DP, TENSOR),
        P(TENSOR, DP),
        P(),
        P(DP, TENSOR),
        P(DP, TENSOR),
        P(TENSOR, DP),
    )
    body = partial(layer, n_dp=sizes[DP], n_tensor=sizes[TENSOR])
    return jax.shard_map(body, mesh=mesh, in_specs=in_specs, out_specs=out_specs, check_vma=False)
```
